512 devices in a mesh: ctx: 64 (over y, z), tp: 8 (over x, core).
Axes of the slice: x: 4, y: 8, z: 8, core: 2. Of those that a mesh axis runs over, the one named last changes fastest.
Arguments:
- query: bfloat16 [8192, 8192], P('ctx', 'tp'), may hold values from -6 to 6
- keyed: bfloat16 [8192, 8192], P('ctx', 'tp'), may hold values from -6 to 6
- valued: bfloat16 [8192, 8192], P('ctx', 'tp'), may hold values from -6 to 6
- short_taps: float32 [3, 3, 8192], P(None, None, 'tp'), may hold values from -3.5 to 3.5
- rates: float32 [8, 8192], P(None, 'tp'), may hold values from 3.0517578e-05 to 0.1
- residues: float32 [8, 8192], P(None, 'tp'), may hold values from -1.5 to 1.5
- skip_gain: float32 [8192], P('tp'), may hold values from -1.6 to 1.6
- doc_ids: int32 [8192], P('ctx'), may hold values from 0 to 7, never falling along the last dimension, each value on 1 to 4096 neighbouring positions
Outputs:
- mixed: bfloat16 [8192, 8192], P('ctx', 'tp')
The draws below stay inside these ranges and needn't reach their ends.
Inputs may be any that keep to these rules, and one draw needn't show every extreme that they name: doc_ids never falls along the sequence; each of the 8 documents holds 1 to 4096 consecutive tokens, one exactly 4096.
All inputs are finite; a program needn't handle non-finite values.
Results may differ from the reference program's by a relative error of at most 0.0065.
Values may be sent and summed in bfloat16 or wider, within the bound.
A program may use at most 128 MiB of HBM per device.

```python
import math
import jax
import jax.numpy as jnp
import numpy as np
from jax import lax

D = 8192
ORDER = 8
SHORT = 3
TOK_DEV = 128
NDOC = 8
TOKENS = 8192
MAXDOC = 4096


def modal_filter(key):
    base_key = jax.random.fold_in(key, 4242)
    kind_key, fast_key, pair_key, spacing_key, slow_key, polarity_key, spread_key, balance_key = jax.random.split(base_key, 8)
    pairs = ORDER // 2
    pair_kind = jax.random.randint(kind_key, (pairs, D), 0, 8)
    mode_kind = jnp.stack([pair_kind, pair_kind], axis=1).reshape(ORDER, D)
    fast_rate = jnp.exp(jax.random.uniform(fast_key, (ORDER, D), jnp.float32, math.log(0.045), math.log(0.1)))
    pair_rate = jnp.exp(jax.random.uniform(pair_key, (pairs, D), jnp.float32, math.log(0.0025), math.log(0.0042)))
    slow_rate = jnp.exp(jax.random.uniform(slow_key, (ORDER, D), jnp.float32, math.log(0.25), math.log(2.0))) / TOKENS
    spread = jax.random.uniform(spread_key, (ORDER, D), jnp.float32, 0.7, 1.3)
    spacing = jax.random.uniform(spacing_key, (pairs, D), jnp.float32, 0.05, 0.12)
    pair_rates = jnp.stack([pair_rate, pair_rate * (1.0 + spacing)], axis=1).reshape(ORDER, D)
    rates = jnp.where(mode_kind < 3, fast_rate, jnp.where(mode_kind < 6, pair_rates, slow_rate))
    polarity = jnp.where(jax.random.randint(polarity_key, (ORDER, D), 0, 2) == 0, -1.0, 1.0)
    fast_res = polarity * jnp.sqrt((1.0 - jnp.exp(-2.0 * fast_rate)) * 0.2) * spread
    amplitude = jnp.sqrt(4.0 * pair_rate * 0.16 * (1.0 + spacing) * (1.0 + 0.5 * spacing)) / spacing
    amplitude = amplitude * jnp.clip(spread[0::2], 0.8, 1.2) * polarity[0::2]
    balance = jax.random.uniform(balance_key, (pairs, D), jnp.float32, 0.97, 1.03)
    pair_res = jnp.stack([amplitude, -amplitude * balance], axis=1).reshape(ORDER, D)
    slow_res = polarity * jnp.sqrt(0.12 / MAXDOC) * spread
    residues = jnp.where(mode_kind < 3, fast_res, jnp.where(mode_kind < 6, pair_res, slow_res))
    return (rates, residues)


def draw_rates(key, part):
    return modal_filter(key)[0].astype(jnp.float32)


def draw_residues(key, part):
    return modal_filter(key)[1].astype(jnp.float32)


def block_levels(rng, shape, pieces, low, high):
    gain, own = 1.0, jax.random.fold_in(rng, 6)
    for position, parts in pieces:
        draws = jnp.exp(jax.random.uniform(jax.random.fold_in(own, position), (parts,), jnp.float32, low / len(pieces), high / len(pieces)))
        gain = gain * jnp.repeat(draws, shape[position] // parts).reshape([-1 if axis == position else 1 for axis in range(len(shape))])
    return gain


def length_profile(number_of, total, most, lean):
    loads = [(1 << 20) // math.isqrt(standing ** lean) + 1 for standing in range(2, number_of + 1)]
    surplus, counts = total - most - (number_of - 1), [1] * (number_of - 1)
    while surplus > 0:
        candidates = [i for i in range(number_of - 1) if counts[i] < most]
        mass, budget = sum([loads[i] for i in candidates]), surplus
        for i in candidates:
            addition = min(most - counts[i], max(1, budget * loads[i] // mass), surplus)
            counts[i] = counts[i] + addition
            surplus = surplus - addition
    return np.array([most] + counts)


def uneven_parts(stream_key, number_of, total, most, slope):
    if number_of == 2:
        one = jax.random.randint(stream_key, (), max(1, total - most), min(most, total - 1) + 1)
        return jnp.stack([one, total - one])
    tallies = jnp.asarray(length_profile(number_of, total, most, slope), jnp.int32)
    pairs = (number_of - 1) // 2
    giver, sink = tallies[1:1 + 2 * pairs:2], tallies[2:2 + 2 * pairs:2]
    slack = jnp.minimum(giver - 1, most - sink)
    moved = jax.random.randint(jax.random.fold_in(stream_key, 1), (pairs,), 0, 1 << 20) % (slack + 1)
    tallies = tallies.at[1:1 + 2 * pairs:2].set(giver - moved).at[2:2 + 2 * pairs:2].set(sink + moved)
    return tallies[jax.random.permutation(jax.random.fold_in(stream_key, 2), number_of)]


def normal_values(stream_key, extent, scale, most, cuts=(), held_as=jnp.bfloat16):
    values = scale * jax.random.normal(stream_key, extent, jnp.float32)
    if cuts:
        values = values * block_levels(stream_key, extent, cuts, -0.22, 0.18)
    return jnp.clip(values, -most, most).astype(held_as)


def setup_inputs(seed: int = 0) -> dict:
    key_list = jax.random.split(jax.random.key(seed), 9)
    return {
        "query": normal_values(key_list[0], (TOKENS, D), 1.0, 6.0, ((0, 64), (1, 8))),
        "keyed": normal_values(key_list[1], (TOKENS, D), 1.0, 6.0, ((0, 64), (1, 8))),
        "valued": normal_values(key_list[2], (TOKENS, D), 1.0, 6.0, ((0, 64), (1, 8))),
        "short_taps": normal_values(key_list[3], (3, SHORT, D), SHORT ** -0.5, 3.5, ((2, 8),), jnp.float32),
        "rates": draw_rates(jax.random.fold_in(key_list[8], 71), 0),
        "residues": draw_residues(jax.random.fold_in(key_list[8], 71), 0),
        "skip_gain": normal_values(key_list[6], (D,), 0.4, 1.6, ((0, 8),), jnp.float32),
        "doc_ids": jnp.searchsorted(jnp.cumsum(uneven_parts(key_list[7], NDOC, TOKENS, MAXDOC, 2)), jnp.arange(TOKENS), side="right").astype(jnp.int32),
    }


def short_conv(ext, ids_ext, taps):
    width = taps.shape[1] - 1
    length = ext.shape[1] - width
    total = jnp.zeros((ext.shape[0], length, ext.shape[2]), jnp.float32)
    for tap in range(taps.shape[1]):
        seg = ext[:, width - tap:width - tap + length]
        same = (ids_ext[width - tap:width - tap + length] == ids_ext[width:]).astype(jnp.float32)
        total = total + taps[:, tap][:, None, :] * seg * same[None, :, None]
    return total


def mode_terms(gated, ids, rates, residues):
    block = gated.shape[0]
    places = jnp.arange(block, dtype=jnp.float32)
    shifted = places - float(block // 2)
    lower = places[:, None] >= places[None, :]
    mask = (lower & (ids[:, None] == ids[None, :])).astype(jnp.float32)
    channels = gated.shape[1]
    long_part = jnp.zeros((block, channels), jnp.float32)
    ends = []
    for group in range(rates.shape[0] // 4):
        rate = rates[4 * group:4 * group + 4]
        grow = jnp.exp(rate[None] * shifted[:, None, None])
        weighted = (grow * gated[:, None, :]).reshape(block, 4 * channels)
        summed = jnp.dot(mask, weighted, precision=lax.Precision.HIGHEST).reshape(block, 4, channels)
        states = summed * jnp.exp(-rate[None] * shifted[:, None, None])
        long_part = long_part + jnp.sum(residues[4 * group:4 * group + 4][None] * states, axis=1)
        ends.append(states[block - 1])
    return long_part, jnp.concatenate(ends, axis=0)


def incoming(carry, ids, prev_last, rates, residues):
    block = ids.shape[0]
    places = jnp.arange(block, dtype=jnp.float32) + 1.0
    live = (ids == prev_last).astype(jnp.float32)
    total = jnp.zeros((block, rates.shape[1]), jnp.float32)
    for group in range(rates.shape[0] // 4):
        rate = rates[4 * group:4 * group + 4]
        weight = residues[4 * group:4 * group + 4] * carry[4 * group:4 * group + 4]
        total = total + jnp.sum(weight[None] * jnp.exp(-rate[None] * places[:, None, None]), axis=1)
    return total * live[:, None]


def transition(ids, prev_last, rates):
    block = ids.shape[0]
    keep = ((ids[0] == prev_last) & (ids[0] == ids[block - 1])).astype(jnp.float32)
    return jnp.exp(-rates * block) * keep


def reference(query, keyed, valued, short_taps, rates, residues, skip_gain, doc_ids):
    width = SHORT - 1
    blocks = TOKENS // TOK_DEV
    stacked = jnp.stack([query, keyed, valued]).reshape(3, blocks, TOK_DEV, D).transpose(1, 0, 2, 3)
    ids_blocks = doc_ids.reshape(blocks, TOK_DEV)

    def step(carry, inputs):
        state, prev_rows, prev_ids = carry
        rows, ids = inputs
        ext = jnp.concatenate([prev_rows, rows], axis=1).astype(jnp.float32)
        ids_ext = jnp.concatenate([prev_ids, ids])
        conv = short_conv(ext, ids_ext, short_taps)
        gated = (conv[1] * conv[2]).astype(jnp.bfloat16)
        gated_f = gated.astype(jnp.float32)
        prev_last = prev_ids[width - 1]
        long_part, ends = mode_terms(gated_f, ids, rates, residues)
        long_all = long_part + incoming(state, ids, prev_last, rates, residues)
        mixed = (conv[0] * (long_all + skip_gain[None] * gated_f)).astype(jnp.bfloat16)
        new_state = transition(ids, prev_last, rates) * state + ends
        return (new_state, rows[:, TOK_DEV - width:], ids[TOK_DEV - width:]), mixed

    start = (jnp.zeros((ORDER, D), jnp.float32), jnp.zeros((3, width, D), jnp.bfloat16), jnp.zeros((width,), jnp.int32))
    _, outs = lax.scan(step, start, (stacked, ids_blocks))
    return outs.reshape(TOKENS, D)
```

```python
import functools

import jax
import jax.numpy as jnp
from jax import lax
from jax.experimental import pallas as pl
from jax.experimental.pallas import tpu as pltpu
from jax.sharding import PartitionSpec as P

MESH = pl.DeviceIdType.MESH
F32 = jnp.float32
BF16 = jnp.bfloat16
ROW = 8
REACH = 4
LANES = 128
GROUPS = 8
STEP = 8
CHUNK = 16


def tree_sum(terms):
    while len(terms) > 1:
        terms = [a + b for a, b in zip(terms[::2], terms[1::2])] + terms[len(terms) & ~1 :]
    return terms[0]


def flag(cond):
    return jnp.where(cond, 1.0, 0.0).astype(F32)


def kernel(
    n_ctx, pitch,
    q_hbm, k_hbm, v_hbm, taps_hbm, rates_hbm, resid_hbm, skip_hbm, ids_hbm,
    out_hbm,
    raw, xs, taps_in, rates_in, resid_in, skip_in, ids,
    prm, taps, rate, resid,
    gated, base, live_q, out_x, out_raw,
    halo_out, halo_in, ends_out, ends_in, row_out, row_in, carry_out, carry_in,
    load_sem, store_sem, halo_send, halo_recv, ends_send, ends_recv, row_send, row_recv,
    carry_send, carry_recv,
):
    block = q_hbm.shape[0]
    modes = rates_hbm.shape[0]
    last = block - 1
    me = lax.axis_index("ctx")
    tp = lax.axis_index("tp")
    y, z = me // ROW, lax.rem(me, ROW)
    n_rows = n_ctx // ROW
    root = y * ROW

    def at(device):
        return (device, tp)

    barrier = pltpu.get_barrier_semaphore()

    def greet(device):
        pl.semaphore_signal(barrier, inc=1, device_id=at(device), device_id_type=MESH)

    @pl.when(z == 0)
    def _():
        for peer in range(1, ROW):
            greet(root + peer)
        for back in range(1, REACH + 1):
            @pl.when(y >= back)
            def _():
                greet(root - back * ROW)

    @pl.when(me > 0)
    def _():
        greet(me - 1)

    loads = [
        pltpu.make_async_copy(src, dst, load_sem.at[i])
        for i, (src, dst) in enumerate(
            [
                (k_hbm, raw.at[1]), (v_hbm, raw.at[2]), (q_hbm, raw.at[0]), (ids_hbm, ids),
                (rates_hbm, rates_in), (taps_hbm, taps_in), (resid_hbm, resid_in),
                (skip_hbm, skip_in),
            ]
        )
    ]
    for load in loads:
        load.start()

    for i in (4, 5, 6, 7):
        loads[i].wait()
    for j in range(GROUPS):
        cols = slice(j * LANES, (j + 1) * LANES)
        prm[pl.ds(j * 32, modes), :] = rates_in[:, cols]
        prm[pl.ds(j * 32 + 8, modes), :] = resid_in[:, cols]
        for s in range(3):
            for tap in range(3):
                prm[pl.ds(j * 32 + 16 + 3 * s + tap, 1), :] = taps_in[s, pl.ds(tap, 1), cols]
    for n in range(modes):
        rate[n] = prm[pl.ds(n, GROUPS, stride=32), :]
        resid[n] = prm[pl.ds(8 + n, GROUPS, stride=32), :]
    for i in range(9):
        taps[i] = prm[pl.ds(16 + i, GROUPS, stride=32), :]

    def spread(s):
        for j in range(GROUPS):
            xs[s, pl.ds(j * pitch, block), :] = raw[s, :, j * LANES : (j + 1) * LANES].astype(F32)

    def token(s, t):
        return xs[s, pl.ds(t, GROUPS, stride=pitch), :]

    loads[0].wait()
    spread(1)
    loads[1].wait()
    spread(2)
    loads[2].wait()
    spread(0)
    loads[3].wait()
    for s in range(3):
        halo_out[2 * s] = token(s, last - 1)
        halo_out[2 * s + 1] = token(s, last)
    halo_out[6] = jnp.full((GROUPS, LANES), ids[last - 1].astype(F32), F32)
    halo_out[7] = jnp.full((GROUPS, LANES), ids[last].astype(F32), F32)

    halo = pltpu.make_async_remote_copy(
        src_ref=halo_out, dst_ref=halo_in, send_sem=halo_send, recv_sem=halo_recv,
        device_id=at(lax.rem(me + 1, n_ctx)), device_id_type=MESH,
    )

    def enter():
        rows_ahead = jnp.minimum(REACH, n_rows - 1 - y)
        expected = jnp.where(me < n_ctx - 1, 1, 0) + jnp.where(z == 0, rows_ahead, 1)
        pl.semaphore_wait(barrier, expected)

        @pl.when(me < n_ctx - 1)
        def _():
            halo.start()

    late = (z == 0) | (z == 3)

    @pl.when(jnp.logical_not(late))
    def _():
        enter()

    def ends_step(i, carry):
        k1, k2, v1, v2, *state = carry
        decay = [jnp.exp(-rate[n]) for n in range(modes)]
        t0 = i * STEP
        for d in range(STEP):
            t = t0 + d
            here = ids[t]
            same1 = flag(here == ids[jnp.maximum(t - 1, 0)])
            same2 = flag(here == ids[jnp.maximum(t - 2, 0)])
            ends = flag((here == ids[last]) & (t >= 2))
            k0, v0 = token(1, t), token(2, t)
            kc = taps[3] * k0 + taps[4] * (k1 * same1) + taps[5] * (k2 * same2)
            vc = taps[6] * v0 + taps[7] * (v1 * same1) + taps[8] * (v2 * same2)
            g = (kc * vc).astype(BF16).astype(F32)
            gated[t] = g
            g = g * ends
            state = [decay[n] * state[n] + g for n in range(modes)]
            k1, k2, v1, v2 = k0, k1, v0, v1
        return (k1, k2, v1, v2, *state)

    zero = jnp.zeros((GROUPS, LANES), F32)
    _, _, _, _, *state = lax.fori_loop(0, block // STEP, ends_step, (zero,) * (4 + modes))
    for n in range(modes):
        ends_out[n] = state[n]

    @pl.when(late)
    def _():
        enter()

    @pl.when(me > 0)
    def _():
        halo.wait_recv()

    @pl.when(me == 0)
    def _():
        halo_in[...] = jnp.full(halo_in.shape, -1.0, F32)

    id0, id1 = ids[0].astype(F32), ids[1].astype(F32)
    before2, before1 = halo_in[6], halo_in[7]
    same_01 = flag(ids[0] == ids[1])
    m0_1, m0_2 = flag(before1 == id0), flag(before2 == id0)
    m1_2 = flag(before1 == id1)

    def conv01(s):
        far, near = halo_in[2 * s], halo_in[2 * s + 1]
        x0, x1 = token(s, 0), token(s, 1)
        a, b, c = taps[3 * s], taps[3 * s + 1], taps[3 * s + 2]
        return (
            a * x0 + b * (near * m0_1) + c * (far * m0_2),
            a * x1 + b * (x0 * same_01) + c * (near * m1_2),
        )

    k_0, k_1 = conv01(1)
    v_0, v_1 = conv01(2)
    g0 = (k_0 * v_0).astype(BF16).astype(F32)
    g1 = (k_1 * v_1).astype(BF16).astype(F32)
    gated[0] = g0
    gated[1] = g1
    ends01 = flag(ids[1] == ids[last])
    for n in range(modes):
        first = jnp.exp(-rate[n]) * (g0 * same_01) + g1
        ends_out[n] += jnp.exp(-rate[n] * float(block - 2)) * (first * ends01)
    ends_out[modes] = m0_1 * flag(ids[0] == ids[last])

    to_root = pltpu.make_async_remote_copy(
        src_ref=ends_out, dst_ref=ends_in.at[lax.rem(z + ROW - 1, ROW)], send_sem=ends_send,
        recv_sem=ends_recv, device_id=at(root), device_id_type=MESH,
    )

    @pl.when(z > 0)
    def _():
        to_root.start()

    q_0, q_1 = conv01(0)

    def local_step(i, carry):
        q1, q2, *state = carry
        decay = [jnp.exp(-rate[n]) for n in range(modes)]
        weight = [resid[n] for n in range(modes)]
        t0 = i * STEP
        for d in range(STEP):
            t = t0 + d
            here = ids[t]
            same1 = flag(here == ids[jnp.maximum(t - 1, 0)])
            same2 = flag(here == ids[jnp.maximum(t - 2, 0)])
            q0 = token(0, t)
            qc = taps[0] * q0 + taps[1] * (q1 * same1) + taps[2] * (q2 * same2)
            if d < 2:
                qc = jnp.where(t == d, (q_0, q_1)[d], qc)
            g = gated[t]
            state = [decay[n] * (state[n] * same1) + g for n in range(modes)]
            long = tree_sum([weight[n] * state[n] for n in range(modes)])
            base[t] = qc * (long + skip_in[...] * g)
            live_q[t] = qc * flag(before1 == here.astype(F32))
            q1, q2 = q0, q1
        return (q1, q2, *state)

    lax.fori_loop(0, block // STEP, local_step, (zero,) * (2 + modes))

    row_size = float(ROW * block)

    def row_copy(back):
        return pltpu.make_async_remote_copy(
            src_ref=row_out, dst_ref=row_in.at[back - 1], send_sem=row_send.at[back - 1],
            recv_sem=row_recv.at[back - 1], device_id=at(lax.rem(me + back * ROW, n_ctx)),
            device_id_type=MESH,
        )

    def carry_copy(peer):
        return pltpu.make_async_remote_copy(
            src_ref=carry_out.at[peer - 1], dst_ref=carry_in, send_sem=carry_send,
            recv_sem=carry_recv, device_id=at(root + peer), device_id_type=MESH,
        )

    @pl.when(z == 0)
    def _():
        pltpu.make_async_remote_copy(
            src_ref=ends_in, dst_ref=ends_in, send_sem=ends_send, recv_sem=ends_recv,
            device_id=at(root), device_id_type=MESH,
        ).wait_recv()
        hop = [jnp.exp(-rate[n] * float(block)) for n in range(modes)]
        total = [ends_out[n] for n in range(modes)]
        keep = ends_out[modes]
        for peer in range(1, ROW):
            k = ends_in[peer - 1, modes]
            keep = keep * k
            total = [total[n] * (hop[n] * k) + ends_in[peer - 1, n] for n in range(modes)]
        for n in range(modes):
            row_out[n] = total[n]
        row_out[modes] = keep
        for back in range(1, REACH + 1):
            @pl.when(y + back < n_rows)
            def _():
                row_copy(back).start()

        carry_in[...] = jnp.zeros(carry_in.shape, F32)
        for back in range(REACH, 0, -1):
            @pl.when(y >= back)
            def _():
                row_copy(back).wait_recv()
                k = row_in[back - 1, modes]
                for n in range(modes):
                    decay = jnp.exp(-rate[n] * row_size) * k
                    carry_in[n] = decay * carry_in[n] + row_in[back - 1, n]

        now = [carry_in[n] for n in range(modes)]
        for peer in range(1, ROW):
            src = ends_out if peer == 1 else ends_in.at[peer - 2]
            k = src[modes]
            now = [now[n] * (hop[n] * k) + src[n] for n in range(modes)]
            for n in range(modes):
                carry_out[peer - 1, n] = now[n]
            carry_copy(peer).start()

    @pl.when(z > 0)
    def _():
        carry_copy(1).wait_recv()

    def store(c):
        rows = pl.ds(pl.multiple_of(c * CHUNK, CHUNK), CHUNK)
        return pltpu.make_async_copy(out_raw.at[rows], out_hbm.at[rows], store_sem)

    def out_step(c, part):
        decay = [jnp.exp(-rate[n]) for n in range(modes)]
        for d in range(CHUNK):
            t = c * CHUNK + d
            part = [decay[n] * part[n] for n in range(modes)]
            out_x[pl.ds(t, GROUPS, stride=pitch), :] = base[t] + live_q[t] * tree_sum(list(part))
        for j in range(GROUPS):
            rows = pl.ds(pl.multiple_of(c * CHUNK, CHUNK), CHUNK)
            piece = out_x[pl.ds(j * pitch + pl.multiple_of(c * CHUNK, CHUNK), CHUNK), :]
            out_raw[rows, j * LANES : (j + 1) * LANES] = piece.astype(BF16)
        store(c).start()
        return part

    lax.fori_loop(
        0, block // CHUNK, out_step, [resid[n] * carry_in[n] for n in range(modes)]
    )

    pltpu.make_async_copy(out_raw, out_hbm, store_sem).wait()

    @pl.when(me < n_ctx - 1)
    def _():
        halo.wait_send()

    @pl.when(z > 0)
    def _():
        to_root.wait_send()

    @pl.when(z == 0)
    def _():
        for back in range(1, REACH + 1):
            @pl.when(y + back < n_rows)
            def _():
                row_copy(back).wait_send()
        pltpu.make_async_remote_copy(
            src_ref=carry_out, dst_ref=carry_out, send_sem=carry_send, recv_sem=carry_recv,
            device_id=at(root), device_id_type=MESH,
        ).wait_send()


def on_device(n_ctx, query, keyed, valued, short_taps, rates, residues, skip_gain, doc_ids):
    block, channels = query.shape
    modes = rates.shape[0]
    assert channels == GROUPS * LANES and block % CHUNK == 0 and modes == 8
    pitch = block + 8
    tile = (GROUPS, LANES)
    dma = pltpu.SemaphoreType.DMA
    any_space = pl.BlockSpec(memory_space=pl.ANY)
    return pl.pallas_call(
        functools.partial(kernel, n_ctx, pitch),
        out_shape=jax.ShapeDtypeStruct(query.shape, BF16),
        in_specs=[any_space] * 8,
        out_specs=any_space,
        scratch_shapes=[
            pltpu.VMEM((3, block, channels), BF16),
            pltpu.VMEM((3, GROUPS * pitch, LANES), F32),
            pltpu.VMEM(short_taps.shape, F32),
            pltpu.VMEM(rates.shape, F32),
            pltpu.VMEM(residues.shape, F32),
            pltpu.VMEM(tile, F32),
            pltpu.SMEM((block,), jnp.int32),
            pltpu.VMEM((GROUPS * 32, LANES), F32),
            pltpu.VMEM((9, *tile), F32),
            pltpu.VMEM((modes, *tile), F32),
            pltpu.VMEM((modes, *tile), F32),
            pltpu.VMEM((block, *tile), F32),
            pltpu.VMEM((block, *tile), F32),
            pltpu.VMEM((block, *tile), F32),
            pltpu.VMEM((GROUPS * pitch, LANES), F32),
            pltpu.VMEM((block, channels), BF16),
            pltpu.VMEM((8, *tile), F32),
            pltpu.VMEM((8, *tile), F32),
            pltpu.VMEM((modes + 1, *tile), F32),
            pltpu.VMEM((ROW - 1, modes + 1, *tile), F32),
            pltpu.VMEM((modes + 1, *tile), F32),
            pltpu.VMEM((REACH, modes + 1, *tile), F32),
            pltpu.VMEM((ROW - 1, modes, *tile), F32),
            pltpu.VMEM((modes, *tile), F32),
            dma((8,)),
            dma, dma, dma, dma, dma,
            dma((REACH,)),
            dma((REACH,)),
            dma, dma,
        ],
        compiler_params=pltpu.CompilerParams(
            collective_id=0, has_side_effects=True, vmem_limit_bytes=32 * 1024 * 1024
        ),
    )(
        query, keyed, valued, short_taps, rates, residues,
        skip_gain.reshape(tile), doc_ids,
    )


def solution(mesh):
    return jax.shard_map(
        functools.partial(on_device, mesh.shape["ctx"]),
        mesh=mesh,
        in_specs=(
            P("ctx", "tp"),
            P("ctx", "tp"),
            P("ctx", "tp"),
            P(None, None, "tp"),
            P(None, "tp"),
            P(None, "tp"),
            P("tp"),
            P("ctx"),
        ),
        out_specs=P("ctx", "tp"),
        check_vma=False,
    )
```

```python
import functools

import jax
import jax.numpy as jnp
from jax import lax
from jax.experimental import pallas as pl
from jax.experimental.pallas import tpu as pltpu
from jax.sharding import PartitionSpec as P

MESH = pl.DeviceIdType.MESH
F32 = jnp.float32
BF16 = jnp.bfloat16
ROW = 8
REACH = 4
LANES = 128
GROUPS = 8
STEP = 8
CHUNK = 16
SPLIT = 4


def tree_sum(terms):
    while len(terms) > 1:
        terms = [a + b for a, b in zip(terms[::2], terms[1::2])] + terms[len(terms) & ~1 :]
    return terms[0]


def flag(cond):
    return jnp.where(cond, 1.0, 0.0).astype(F32)


def kernel(
    n_ctx, pitch,
    q_hbm, k_hbm, v_hbm, taps_hbm, rates_hbm, resid_hbm, skip_hbm, ids_hbm,
    out,
    raw, xs, taps_in, rates_in, resid_in, skip_in, ids,
    prm, taps, rate, resid,
    gated, base, live_q, out_x,
    tail_out, tail_in, tail_q_out, tail_q_in, head_out, head_in,
    ends_out, ends_in, relay, row_out, row_in, carry_out, carry_in,
    load_sem, tail_sems, tail_q_sems, head_sems, lift_sems, forward_send, ends_sems,
    row_send, row_recv, carry_sems,
):
    block = q_hbm.shape[0]
    modes = rates_hbm.shape[0]
    last = block - 1
    me = lax.axis_index("ctx")
    tp = lax.axis_index("tp")
    y, z = me // ROW, lax.rem(me, ROW)
    n_rows = n_ctx // ROW
    root = y * ROW

    def at(device):
        return (device, tp)

    def remote(src, dst, send, recv, device):
        return pltpu.make_async_remote_copy(
            src_ref=src, dst_ref=dst, send_sem=send, recv_sem=recv,
            device_id=at(device), device_id_type=MESH,
        )

    barrier = pltpu.get_barrier_semaphore()

    def greet(device):
        pl.semaphore_signal(barrier, inc=1, device_id=at(device), device_id_type=MESH)

    @pl.when(z == 0)
    def _():
        for peer in range(1, ROW):
            if peer != SPLIT:
                greet(root + peer)
        for back in range(1, REACH + 1):
            @pl.when(y >= back)
            def _():
                greet(root - back * ROW)

    @pl.when(z == SPLIT - 1)
    def _():
        greet(me + 1)

    @pl.when(me > 0)
    def _():
        greet(me - 1)

    loads = [
        pltpu.make_async_copy(src, dst, load_sem.at[i])
        for i, (src, dst) in enumerate(
            [
                (k_hbm, raw.at[1]), (v_hbm, raw.at[2]), (ids_hbm, ids), (rates_hbm, rates_in),
                (taps_hbm, taps_in), (q_hbm, raw.at[0]), (resid_hbm, resid_in),
                (skip_hbm, skip_in),
            ]
        )
    ]
    for load in loads:
        load.start()

    def spread(s):
        for j in range(GROUPS):
            xs[s, pl.ds(j * pitch, block), :] = raw[s, :, j * LANES : (j + 1) * LANES].astype(F32)

    def token(s, t):
        return xs[s, pl.ds(t, GROUPS, stride=pitch), :]

    def splat(value):
        return jnp.full((GROUPS, LANES), value.astype(F32), F32)

    def put(ref, i, first, second):
        ref[i] = jnp.concatenate([first, second], axis=0).astype(BF16)

    def get(ref, i):
        both = ref[i].astype(F32)
        return both[:GROUPS], both[GROUPS:]

    loads[0].wait()
    spread(1)
    loads[1].wait()
    spread(2)
    loads[2].wait()
    id_0, id_1, id_end = splat(ids[0]), splat(ids[1]), splat(ids[last])
    for s in (1, 2):
        put(tail_out, s - 1, token(s, last - 1), token(s, last))
        put(head_out, s - 1, token(s, 0), token(s, 1))
    put(tail_out, 2, splat(ids[last - 1]), id_end)
    put(head_out, 2, id_0, id_1)
    put(head_out, 3, id_end, id_end)

    following = lax.rem(me + 1, n_ctx)
    tail = remote(tail_out, tail_in, tail_sems.at[0], tail_sems.at[1], following)
    tail_q = remote(tail_q_out, tail_q_in, tail_q_sems.at[0], tail_q_sems.at[1], following)

    def enter():
        rows_ahead = jnp.minimum(REACH, n_rows - 1 - y)
        expected = jnp.where(me < n_ctx - 1, 1, 0) + jnp.where(z == 0, rows_ahead, 1)
        pl.semaphore_wait(barrier, expected)

        @pl.when(me < n_ctx - 1)
        def _():
            tail.start()

    late = (z == 0) | (z == SPLIT - 1)

    @pl.when(jnp.logical_not(late))
    def _():
        enter()

    loads[3].wait()
    loads[4].wait()
    for j in range(GROUPS):
        cols = slice(j * LANES, (j + 1) * LANES)
        prm[pl.ds(j * 32, modes), :] = rates_in[:, cols]
        for s in range(3):
            for tap in range(3):
                prm[pl.ds(j * 32 + 16 + 3 * s + tap, 1), :] = taps_in[s, pl.ds(tap, 1), cols]
    for n in range(modes):
        rate[n] = prm[pl.ds(n, GROUPS, stride=32), :]
    for i in range(9):
        taps[i] = prm[pl.ds(16 + i, GROUPS, stride=32), :]

    def ends_step(i, carry):
        k1, k2, v1, v2, *state = carry
        decay = [jnp.exp(-rate[n]) for n in range(modes)]
        t0 = i * STEP
        for d in range(STEP):
            t = t0 + d
            here = ids[t]
            same1 = flag(here == ids[jnp.maximum(t - 1, 0)])
            same2 = flag(here == ids[jnp.maximum(t - 2, 0)])
            ends = flag((here == ids[last]) & (t >= 2))
            k0, v0 = token(1, t), token(2, t)
            kc = taps[3] * k0 + taps[4] * (k1 * same1) + taps[5] * (k2 * same2)
            vc = taps[6] * v0 + taps[7] * (v1 * same1) + taps[8] * (v2 * same2)
            g = (kc * vc).astype(BF16).astype(F32)
            gated[t] = g
            g = g * ends
            state = [decay[n] * state[n] + g for n in range(modes)]
            k1, k2, v1, v2 = k0, k1, v0, v1
        return (k1, k2, v1, v2, *state)

    zero = jnp.zeros((GROUPS, LANES), F32)
    _, _, _, _, *state = lax.fori_loop(0, block // STEP, ends_step, (zero,) * (4 + modes))
    for n in range(modes):
        ends_out[n] = state[n]
    ends_out[modes] = zero

    @pl.when(late)
    def _():
        enter()

    lifter = root + SPLIT - 1
    head = remote(head_out, head_in, head_sems.at[0], head_sems.at[1], lifter)
    lift = remote(ends_out, relay, lift_sems.at[0], lift_sems.at[1], lifter)
    forward = remote(relay, ends_in.at[SPLIT - 1], forward_send, ends_sems.at[1], root)
    slot = lax.rem(z + ROW - 1, ROW)
    ends = remote(ends_out, ends_in.at[slot], ends_sems.at[0], ends_sems.at[1], root)

    @pl.when(z == SPLIT)
    def _():
        head.start()
        lift.start()

    def first_two(s, before, x0, x1, before_ids, id0, id1):
        far, near = before
        id_far, id_near = before_ids
        a, b, c = taps[3 * s], taps[3 * s + 1], taps[3 * s + 2]
        return (
            a * x0 + b * (near * flag(id_near == id0)) + c * (far * flag(id_far == id0)),
            a * x1 + b * (x0 * flag(id0 == id1)) + c * (near * flag(id_near == id1)),
        )

    def first_gated(tail_ref, xk, xv, id0, id1):
        before_ids = get(tail_ref, 2)
        k = first_two(1, get(tail_ref, 0), *xk, before_ids, id0, id1)
        v = first_two(2, get(tail_ref, 1), *xv, before_ids, id0, id1)
        return [(a * b).astype(BF16).astype(F32) for a, b in zip(k, v)]

    def add_first(ref, g, id_near, id0, id1, end_id):
        joined, ending = flag(id0 == id1), flag(id1 == end_id)
        for n in range(modes):
            first = jnp.exp(-rate[n]) * (g[0] * joined) + g[1]
            ref[n] += jnp.exp(-rate[n] * float(block - 2)) * (first * ending)
        ref[modes] = flag(id_near == id0) * flag(id0 == end_id)

    def own_first():
        _, near_id = get(tail_in, 2)
        xk, xv = [(token(s, 0), token(s, 1)) for s in (1, 2)]
        gated[0], gated[1] = g = first_gated(tail_in, xk, xv, id_0, id_1)
        return g, near_id, id_0, id_1, id_end

    prompt = (z != 0) & (z != SPLIT)

    @pl.when(prompt)
    def _():
        tail.wait_recv()
        add_first(ends_out, *own_first())
        ends.start()

    loads[5].wait()
    spread(0)
    put(tail_q_out, 0, token(0, last - 1), token(0, last))

    @pl.when(me < n_ctx - 1)
    def _():
        tail_q.start()

    loads[6].wait()
    loads[7].wait()
    for j in range(GROUPS):
        prm[pl.ds(j * 32 + 8, modes), :] = resid_in[:, j * LANES : (j + 1) * LANES]
    for n in range(modes):
        resid[n] = prm[pl.ds(8 + n, GROUPS, stride=32), :]

    def local_step(i, carry):
        q1, q2, *state = carry
        decay = [jnp.exp(-rate[n]) for n in range(modes)]
        weight = [resid[n] for n in range(modes)]
        t0 = i * STEP
        for d in range(STEP):
            t = t0 + d
            here = ids[t]
            same1 = flag(here == ids[jnp.maximum(t - 1, 0)])
            same2 = flag(here == ids[jnp.maximum(t - 2, 0)])
            q0 = token(0, t)
            qc = taps[0] * q0 + taps[1] * (q1 * same1) + taps[2] * (q2 * same2)
            g = gated[t]
            if d < 2:
                g = g * flag(t >= 2)
            state = [decay[n] * (state[n] * same1) + g for n in range(modes)]
            long = tree_sum([weight[n] * state[n] for n in range(modes)])
            base[t] = qc * (long + skip_in[...] * g)
            live_q[t] = qc * flag(here == ids[1])
            q1, q2 = q0, q1
        return (q1, q2, *state)

    lax.fori_loop(0, block // STEP, local_step, (zero,) * (2 + modes))

    @pl.when((z == SPLIT) | ((z == 0) & (me > 0)))
    def _():
        tail.wait_recv()

    @pl.when(me == 0)
    def _():
        tail_in[...] = jnp.full(tail_in.shape, -1.0, BF16)
        tail_q_in[...] = jnp.zeros(tail_q_in.shape, BF16)

    @pl.when(z == 0)
    def _():
        add_first(ends_out, *own_first())

    @pl.when(z == SPLIT)
    def _():
        own_first()

    @pl.when(z == SPLIT - 1)
    def _():
        head.wait_recv()
        lift.wait_recv()
        (head_0, head_1), (head_end, _) = get(head_in, 2), get(head_in, 3)
        first = first_gated(tail_out, get(head_in, 0), get(head_in, 1), head_0, head_1)
        add_first(relay, first, id_end, head_0, head_1, head_end)
        forward.start()

    @pl.when(me > 0)
    def _():
        tail_q.wait_recv()

    row_size = float(ROW * block)

    def row_copy(back):
        return remote(
            row_out, row_in.at[back - 1], row_send.at[back - 1], row_recv.at[back - 1],
            lax.rem(me + back * ROW, n_ctx),
        )

    def carry_copy(peer):
        return remote(
            carry_out.at[peer - 1], carry_in, carry_sems.at[0], carry_sems.at[1], root + peer
        )

    def all_of(ref, sems):
        return remote(ref, ref, sems.at[0], sems.at[1], root)

    @pl.when(z == 0)
    def _():
        all_of(ends_in, ends_sems).wait_recv()
        hop = [jnp.exp(-rate[n] * float(block)) for n in range(modes)]
        leap = [jnp.exp(-rate[n] * row_size) for n in range(modes)]
        total = [ends_out[n] for n in range(modes)]
        keep = ends_out[modes]
        for peer in range(1, ROW):
            k = ends_in[peer - 1, modes]
            keep = keep * k
            total = [total[n] * (hop[n] * k) + ends_in[peer - 1, n] for n in range(modes)]
        for n in range(modes):
            row_out[n] = total[n]
        row_out[modes] = keep

        for back in range(REACH, 0, -1):
            @pl.when(y + back < n_rows)
            def _():
                row_copy(back).start()

        carry_in[...] = jnp.zeros(carry_in.shape, F32)
        for back in range(REACH, 0, -1):
            @pl.when(y >= back)
            def _():
                row_copy(back).wait_recv()
                for n in range(modes):
                    carry_in[n] = (
                        leap[n] * row_in[back - 1, modes] * carry_in[n] + row_in[back - 1, n]
                    )

        now = [carry_in[n] for n in range(modes)]
        for peer in range(1, ROW):
            src = ends_out if peer == 1 else ends_in.at[peer - 2]
            k = src[modes]
            now = [now[n] * (hop[n] * k) + src[n] for n in range(modes)]
            for n in range(modes):
                carry_out[peer - 1, n] = now[n]
            carry_copy(peer).start()

    @pl.when(z > 0)
    def _():
        carry_copy(1).wait_recv()

    before_ids = get(tail_in, 2)
    q_first = first_two(0, get(tail_q_in, 0), token(0, 0), token(0, 1), before_ids, id_0, id_1)
    state = [carry_in[n] * flag(before_ids[1] == id_0) for n in range(modes)]
    for t in (0, 1):
        if t == 1:
            joined = flag(id_0 == id_1)
            state = [state[n] * joined for n in range(modes)]
        state = [jnp.exp(-rate[n]) * state[n] + gated[t] for n in range(modes)]
        long = tree_sum([resid[n] * state[n] for n in range(modes)])
        base[t] = q_first[t] * (long + skip_in[...] * gated[t])
        live_q[t] = zero

    def out_step(c, part):
        decay = [jnp.exp(-rate[n]) for n in range(modes)]
        for d in range(CHUNK):
            t = c * CHUNK + d
            part = [decay[n] * part[n] for n in range(modes)]
            out_x[pl.ds(t, GROUPS, stride=pitch), :] = base[t] + live_q[t] * tree_sum(list(part))
        for j in range(GROUPS):
            rows = pl.ds(pl.multiple_of(c * CHUNK, CHUNK), CHUNK)
            piece = out_x[pl.ds(j * pitch + pl.multiple_of(c * CHUNK, CHUNK), CHUNK), :]
            out[rows, j * LANES : (j + 1) * LANES] = piece.astype(BF16)
        return part

    lax.fori_loop(
        0, block // CHUNK, out_step, [resid[n] * jnp.exp(2.0 * rate[n]) * state[n] for n in range(modes)]
    )

    @pl.when(me < n_ctx - 1)
    def _():
        tail.wait_send()
        tail_q.wait_send()

    @pl.when(z == SPLIT - 1)
    def _():
        forward.wait_send()

    @pl.when(z == SPLIT)
    def _():
        head.wait_send()
        lift.wait_send()

    @pl.when(prompt)
    def _():
        ends.wait_send()

    @pl.when(z == 0)
    def _():
        for back in range(1, REACH + 1):
            @pl.when(y + back < n_rows)
            def _():
                row_copy(back).wait_send()

        all_of(carry_out, carry_sems).wait_send()


def on_device(n_ctx, query, keyed, valued, short_taps, rates, residues, skip_gain, doc_ids):
    block, channels = query.shape
    modes = rates.shape[0]
    assert channels == GROUPS * LANES and block % CHUNK == 0 and modes == 8
    pitch = block + 8
    tile, twice = (GROUPS, LANES), (2 * GROUPS, LANES)
    dma = pltpu.SemaphoreType.DMA
    hbm = pl.BlockSpec(memory_space=pltpu.HBM)
    return pl.pallas_call(
        functools.partial(kernel, n_ctx, pitch),
        out_shape=pltpu.VMEM(query.shape, BF16),
        in_specs=[hbm] * 8,
        out_specs=pl.BlockSpec(memory_space=pltpu.VMEM),
        scratch_shapes=[
            pltpu.VMEM((3, block, channels), BF16),
            pltpu.VMEM((3, GROUPS * pitch, LANES), F32),
            pltpu.VMEM(short_taps.shape, F32),
            pltpu.VMEM(rates.shape, F32),
            pltpu.VMEM(residues.shape, F32),
            pltpu.VMEM(tile, F32),
            pltpu.SMEM((block,), jnp.int32),
            pltpu.VMEM((GROUPS * 32, LANES), F32),
            pltpu.VMEM((9, *tile), F32),
            pltpu.VMEM((modes, *tile), F32),
            pltpu.VMEM((modes, *tile), F32),
            pltpu.VMEM((block, *tile), F32),
            pltpu.VMEM((block, *tile), F32),
            pltpu.VMEM((block, *tile), F32),
            pltpu.VMEM((GROUPS * pitch, LANES), F32),
            pltpu.VMEM((3, *twice), BF16),
            pltpu.VMEM((3, *twice), BF16),
            pltpu.VMEM((1, *twice), BF16),
            pltpu.VMEM((1, *twice), BF16),
            pltpu.VMEM((4, *twice), BF16),
            pltpu.VMEM((4, *twice), BF16),
            pltpu.VMEM((modes + 1, *tile), F32),
            pltpu.VMEM((ROW - 1, modes + 1, *tile), F32),
            pltpu.VMEM((modes + 1, *tile), F32),
            pltpu.VMEM((modes + 1, *tile), F32),
            pltpu.VMEM((REACH, modes + 1, *tile), F32),
            pltpu.VMEM((ROW - 1, modes, *tile), F32),
            pltpu.VMEM((modes, *tile), F32),
            dma((8,)),
            dma((2,)),
            dma((2,)),
            dma((2,)),
            dma((2,)),
            dma,
            dma((2,)),
            dma((REACH,)),
            dma((REACH,)),
            dma((2,)),
        ],
        compiler_params=pltpu.CompilerParams(
            collective_id=0, has_side_effects=True, vmem_limit_bytes=60 * 1024 * 1024
        ),
    )(
        query, keyed, valued, short_taps, rates, residues,
        skip_gain.reshape(tile), doc_ids,
    )


def solution(mesh):
    return jax.shard_map(
        functools.partial(on_device, mesh.shape["ctx"]),
        mesh=mesh,
        in_specs=(
            P("ctx", "tp"),
            P("ctx", "tp"),
            P("ctx", "tp"),
            P(None, None, "tp"),
            P(None, "tp"),
            P(None, "tp"),
            P("tp"),
            P("ctx"),
        ),
        out_specs=P("ctx", "tp"),
        check_vma=False,
    )
```

```python
import functools

import jax
import jax.numpy as jnp
from jax import lax
from jax.experimental import pallas as pl
from jax.experimental.pallas import tpu as pltpu
from jax.sharding import PartitionSpec as P

MESH = pl.DeviceIdType.MESH
F32 = jnp.float32
BF16 = jnp.bfloat16
ROW = 8
REACH = 4
LANES = 128
GROUPS = 8
STEP = 8
CHUNK = 64
SPLIT = 4


def tree_sum(terms):
    while len(terms) > 1:
        terms = [a + b for a, b in zip(terms[::2], terms[1::2])] + terms[len(terms) & ~1 :]
    return terms[0]


def flag(cond):
    return jnp.where(cond, 1.0, 0.0).astype(F32)


def kernel(
    n_ctx, pitch,
    q_hbm, k_hbm, v_hbm, taps_hbm, rates_hbm, resid_hbm, skip_hbm, ids_hbm,
    out,
    raw, xs, taps_in, rates_in, resid_in, skip_in, ids,
    prm, taps, rate, resid, power,
    gated, base, live_q, out_x,
    tail_out, tail_in, tail_q_out, tail_q_in, head_out, head_in,
    ends_out, ends_in, relay, row_out, row_in, carry_out, carry_in,
    load_sem, tail_sems, tail_q_sems, head_sems, lift_sems, forward_send, ends_sems,
    row_send, row_recv, carry_sems,
):
    block = q_hbm.shape[0]
    modes = rates_hbm.shape[0]
    last = block - 1
    me = lax.axis_index("ctx")
    tp = lax.axis_index("tp")
    y, z = me // ROW, lax.rem(me, ROW)
    n_rows = n_ctx // ROW
    root = y * ROW

    def at(device):
        return (device, tp)

    def remote(src, dst, send, recv, device):
        return pltpu.make_async_remote_copy(
            src_ref=src, dst_ref=dst, send_sem=send, recv_sem=recv,
            device_id=at(device), device_id_type=MESH,
        )

    barrier = pltpu.get_barrier_semaphore()

    def greet(device):
        pl.semaphore_signal(barrier, inc=1, device_id=at(device), device_id_type=MESH)

    @pl.when(z == 0)
    def _():
        for peer in range(1, ROW):
            if peer != SPLIT:
                greet(root + peer)
        for back in range(1, REACH + 1):
            @pl.when(y >= back)
            def _():
                greet(root - back * ROW)

    @pl.when(z == SPLIT - 1)
    def _():
        greet(me + 1)

    @pl.when(me > 0)
    def _():
        greet(me - 1)

    loads = [
        pltpu.make_async_copy(src, dst, load_sem.at[i])
        for i, (src, dst) in enumerate(
            [
                (k_hbm, raw.at[1]), (v_hbm, raw.at[2]), (ids_hbm, ids), (rates_hbm, rates_in),
                (taps_hbm, taps_in), (q_hbm, raw.at[0]), (resid_hbm, resid_in),
                (skip_hbm, skip_in),
            ]
        )
    ]
    for load in loads:
        load.start()

    def spread(s):
        for j in range(GROUPS):
            xs[s, pl.ds(j * pitch, block), :] = raw[s, :, j * LANES : (j + 1) * LANES].astype(F32)

    def token(s, t):
        return xs[s, pl.ds(t, GROUPS, stride=pitch), :]

    def splat(value):
        return jnp.full((GROUPS, LANES), value.astype(F32), F32)

    def put(ref, i, first, second):
        ref[i] = jnp.concatenate([first, second], axis=0).astype(BF16)

    def get(ref, i):
        both = ref[i].astype(F32)
        return both[:GROUPS], both[GROUPS:]

    loads[0].wait()
    spread(1)
    loads[1].wait()
    spread(2)
    loads[2].wait()
    id_0, id_1, id_end = splat(ids[0]), splat(ids[1]), splat(ids[last])
    for s in (1, 2):
        put(tail_out, s - 1, token(s, last - 1), token(s, last))
        put(head_out, s - 1, token(s, 0), token(s, 1))
    put(tail_out, 2, splat(ids[last - 1]), id_end)
    put(head_out, 2, id_0, id_1)
    put(head_out, 3, id_end, id_end)

    following = lax.rem(me + 1, n_ctx)
    tail = remote(tail_out, tail_in, tail_sems.at[0], tail_sems.at[1], following)
    tail_q = remote(tail_q_out, tail_q_in, tail_q_sems.at[0], tail_q_sems.at[1], following)

    def enter():
        rows_ahead = jnp.minimum(REACH, n_rows - 1 - y)
        expected = jnp.where(me < n_ctx - 1, 1, 0) + jnp.where(z == 0, rows_ahead, 1)
        pl.semaphore_wait(barrier, expected)

        @pl.when(me < n_ctx - 1)
        def _():
            tail.start()

    late = (z == 0) | (z == SPLIT - 1)

    @pl.when(jnp.logical_not(late))
    def _():
        enter()

    loads[3].wait()
    loads[4].wait()
    for j in range(GROUPS):
        cols = slice(j * LANES, (j + 1) * LANES)
        prm[pl.ds(j * 32, modes), :] = rates_in[:, cols]
        for s in range(3):
            for tap in range(3):
                prm[pl.ds(j * 32 + 16 + 3 * s + tap, 1), :] = taps_in[s, pl.ds(tap, 1), cols]
    for n in range(modes):
        rate[n] = prm[pl.ds(n, GROUPS, stride=32), :]
        power[0, n] = jnp.exp(-rate[n])
    for i in range(9):
        taps[i] = prm[pl.ds(16 + i, GROUPS, stride=32), :]

    def ends_step(i, carry):
        k1, k2, v1, v2, *state = carry
        decay = [power[0, n] for n in range(modes)]
        t0 = i * STEP
        for d in range(STEP):
            t = t0 + d
            here = ids[t]
            same1 = flag(here == ids[jnp.maximum(t - 1, 0)])
            same2 = flag(here == ids[jnp.maximum(t - 2, 0)])
            ends = flag((here == ids[last]) & (t >= 2))
            k0, v0 = token(1, t), token(2, t)
            kc = taps[3] * k0 + taps[4] * (k1 * same1) + taps[5] * (k2 * same2)
            vc = taps[6] * v0 + taps[7] * (v1 * same1) + taps[8] * (v2 * same2)
            g = (kc * vc).astype(BF16).astype(F32)
            gated[t] = g
            g = g * ends
            state = [decay[n] * state[n] + g for n in range(modes)]
            k1, k2, v1, v2 = k0, k1, v0, v1
        return (k1, k2, v1, v2, *state)

    zero = jnp.zeros((GROUPS, LANES), F32)
    _, _, _, _, *state = lax.fori_loop(0, block // STEP, ends_step, (zero,) * (4 + modes))
    for n in range(modes):
        ends_out[n] = state[n]
    ends_out[modes] = zero
    for i, steps in ((1, block - 2), (2, block), (3, ROW * block)):
        for n in range(modes):
            power[i, n] = jnp.exp(-rate[n] * float(steps))

    @pl.when(late)
    def _():
        enter()

    lifter = root + SPLIT - 1
    head = remote(head_out, head_in, head_sems.at[0], head_sems.at[1], lifter)
    lift = remote(ends_out, relay, lift_sems.at[0], lift_sems.at[1], lifter)
    forward = remote(relay, ends_in.at[SPLIT - 1], forward_send, ends_sems.at[1], root)
    slot = lax.rem(z + ROW - 1, ROW)
    ends = remote(ends_out, ends_in.at[slot], ends_sems.at[0], ends_sems.at[1], root)

    @pl.when(z == SPLIT)
    def _():
        head.start()
        lift.start()

    def first_two(s, before, x0, x1, before_ids, id0, id1):
        far, near = before
        id_far, id_near = before_ids
        a, b, c = taps[3 * s], taps[3 * s + 1], taps[3 * s + 2]
        return (
            a * x0 + b * (near * flag(id_near == id0)) + c * (far * flag(id_far == id0)),
            a * x1 + b * (x0 * flag(id0 == id1)) + c * (near * flag(id_near == id1)),
        )

    def first_gated(tail_ref, xk, xv, id0, id1):
        before_ids = get(tail_ref, 2)
        k = first_two(1, get(tail_ref, 0), *xk, before_ids, id0, id1)
        v = first_two(2, get(tail_ref, 1), *xv, before_ids, id0, id1)
        return [(a * b).astype(BF16).astype(F32) for a, b in zip(k, v)]

    def add_first(ref, g, id_near, id0, id1, end_id):
        joined, ending = flag(id0 == id1), flag(id1 == end_id)
        for n in range(modes):
            first = power[0, n] * (g[0] * joined) + g[1]
            ref[n] += power[1, n] * (first * ending)
        ref[modes] = flag(id_near == id0) * flag(id0 == end_id)

    def own_first():
        _, near_id = get(tail_in, 2)
        xk, xv = [(token(s, 0), token(s, 1)) for s in (1, 2)]
        gated[0], gated[1] = g = first_gated(tail_in, xk, xv, id_0, id_1)
        return g, near_id, id_0, id_1, id_end

    prompt = (z != 0) & (z != SPLIT)

    @pl.when(prompt)
    def _():
        tail.wait_recv()
        add_first(ends_out, *own_first())
        ends.start()

    loads[5].wait()
    spread(0)
    put(tail_q_out, 0, token(0, last - 1), token(0, last))

    @pl.when(me < n_ctx - 1)
    def _():
        tail_q.start()

    loads[6].wait()
    loads[7].wait()
    for j in range(GROUPS):
        prm[pl.ds(j * 32 + 8, modes), :] = resid_in[:, j * LANES : (j + 1) * LANES]
    for n in range(modes):
        resid[n] = prm[pl.ds(8 + n, GROUPS, stride=32), :]

    def local_step(i, carry):
        q1, q2, *state = carry
        decay = [power[0, n] for n in range(modes)]
        weight = [resid[n] for n in range(modes)]
        t0 = i * STEP
        for d in range(STEP):
            t = t0 + d
            here = ids[t]
            same1 = flag(here == ids[jnp.maximum(t - 1, 0)])
            same2 = flag(here == ids[jnp.maximum(t - 2, 0)])
            q0 = token(0, t)
            qc = taps[0] * q0 + taps[1] * (q1 * same1) + taps[2] * (q2 * same2)
            g = gated[t]
            if d < 2:
                g = g * flag(t >= 2)
            state = [decay[n] * (state[n] * same1) + g for n in range(modes)]
            long = tree_sum([weight[n] * state[n] for n in range(modes)])
            base[t] = qc * (long + skip_in[...] * g)
            live_q[t] = qc * flag(here == ids[1])
            q1, q2 = q0, q1
        return (q1, q2, *state)

    lax.fori_loop(0, block // STEP, local_step, (zero,) * (2 + modes))

    @pl.when((z == SPLIT) | ((z == 0) & (me > 0)))
    def _():
        tail.wait_recv()

    @pl.when(me == 0)
    def _():
        tail_in[...] = jnp.full(tail_in.shape, -1.0, BF16)
        tail_q_in[...] = jnp.zeros(tail_q_in.shape, BF16)

    @pl.when(z == 0)
    def _():
        add_first(ends_out, *own_first())

    @pl.when(z == SPLIT)
    def _():
        own_first()

    @pl.when(z == SPLIT - 1)
    def _():
        head.wait_recv()
        lift.wait_recv()
        (head_0, head_1), (head_end, _) = get(head_in, 2), get(head_in, 3)
        first = first_gated(tail_out, get(head_in, 0), get(head_in, 1), head_0, head_1)
        add_first(relay, first, id_end, head_0, head_1, head_end)
        forward.start()

    @pl.when(me > 0)
    def _():
        tail_q.wait_recv()

    def row_copy(back):
        return remote(
            row_out, row_in.at[back - 1], row_send.at[back - 1], row_recv.at[back - 1],
            lax.rem(me + back * ROW, n_ctx),
        )

    def carry_copy(peer):
        return remote(
            carry_out.at[peer - 1], carry_in, carry_sems.at[0], carry_sems.at[1], root + peer
        )

    def all_of(ref, sems):
        return remote(ref, ref, sems.at[0], sems.at[1], root)

    @pl.when(z == 0)
    def _():
        all_of(ends_in, ends_sems).wait_recv()
        hop = [power[2, n] for n in range(modes)]
        leap = [power[3, n] for n in range(modes)]
        total = [ends_out[n] for n in range(modes)]
        keep = ends_out[modes]
        for peer in range(1, ROW):
            k = ends_in[peer - 1, modes]
            keep = keep * k
            total = [total[n] * (hop[n] * k) + ends_in[peer - 1, n] for n in range(modes)]
        for n in range(modes):
            row_out[n] = total[n]
        row_out[modes] = keep

        orders = {0: (1, 2, 3, 4), 1: (1, 2, 4, 3), 2: (4, 1, 3, 2), 3: (4, 3, 2, 1)}
        for at_row in range(n_rows):
            @pl.when(y == at_row)
            def _():
                for back in orders.get(at_row, (3, 2, 1)):
                    if at_row + back < n_rows:
                        row_copy(back).start()

        carry_in[...] = jnp.zeros(carry_in.shape, F32)
        for back in range(REACH, 0, -1):
            @pl.when(y >= back)
            def _():
                row_copy(back).wait_recv()
                for n in range(modes):
                    carry_in[n] = (
                        leap[n] * row_in[back - 1, modes] * carry_in[n] + row_in[back - 1, n]
                    )

        now = [carry_in[n] for n in range(modes)]
        for peer in range(1, ROW):
            src = ends_out if peer == 1 else ends_in.at[peer - 2]
            k = src[modes]
            now = [now[n] * (hop[n] * k) + src[n] for n in range(modes)]
            for n in range(modes):
                carry_out[peer - 1, n] = now[n]
            carry_copy(peer).start()

    @pl.when(z > 0)
    def _():
        carry_copy(1).wait_recv()

    before_ids = get(tail_in, 2)
    q_first = first_two(0, get(tail_q_in, 0), token(0, 0), token(0, 1), before_ids, id_0, id_1)
    state = [carry_in[n] * flag(before_ids[1] == id_0) for n in range(modes)]
    for t in (0, 1):
        if t == 1:
            joined = flag(id_0 == id_1)
            state = [state[n] * joined for n in range(modes)]
        state = [power[0, n] * state[n] + gated[t] for n in range(modes)]
        long = tree_sum([resid[n] * state[n] for n in range(modes)])
        base[t] = q_first[t] * (long + skip_in[...] * gated[t])
        live_q[t] = zero

    def out_step(c, part):
        decay = [power[0, n] for n in range(modes)]
        for d in range(CHUNK):
            t = c * CHUNK + d
            part = [decay[n] * part[n] for n in range(modes)]
            out_x[pl.ds(t, GROUPS, stride=pitch), :] = base[t] + live_q[t] * tree_sum(list(part))
        for j in range(GROUPS):
            rows = pl.ds(pl.multiple_of(c * CHUNK, CHUNK), CHUNK)
            piece = out_x[pl.ds(j * pitch + pl.multiple_of(c * CHUNK, CHUNK), CHUNK), :]
            out[rows, j * LANES : (j + 1) * LANES] = piece.astype(BF16)
        return part

    lax.fori_loop(
        0, block // CHUNK, out_step, [resid[n] * jnp.exp(2.0 * rate[n]) * state[n] for n in range(modes)]
    )

    @pl.when(me < n_ctx - 1)
    def _():
        tail.wait_send()
        tail_q.wait_send()

    @pl.when(z == SPLIT - 1)
    def _():
        forward.wait_send()

    @pl.when(z == SPLIT)
    def _():
        head.wait_send()
        lift.wait_send()

    @pl.when(prompt)
    def _():
        ends.wait_send()

    @pl.when(z == 0)
    def _():
        for back in range(1, REACH + 1):
            @pl.when(y + back < n_rows)
            def _():
                row_copy(back).wait_send()

        all_of(carry_out, carry_sems).wait_send()


def on_device(n_ctx, query, keyed, valued, short_taps, rates, residues, skip_gain, doc_ids):
    block, channels = query.shape
    modes = rates.shape[0]
    assert channels == GROUPS * LANES and block % CHUNK == 0 and modes == 8
    pitch = block + 8
    tile, twice = (GROUPS, LANES), (2 * GROUPS, LANES)
    dma = pltpu.SemaphoreType.DMA
    hbm = pl.BlockSpec(memory_space=pltpu.HBM)
    return pl.pallas_call(
        functools.partial(kernel, n_ctx, pitch),
        out_shape=pltpu.VMEM(query.shape, BF16),
        in_specs=[hbm] * 8,
        out_specs=pl.BlockSpec(memory_space=pltpu.VMEM),
        scratch_shapes=[
            pltpu.VMEM((3, block, channels), BF16),
            pltpu.VMEM((3, GROUPS * pitch, LANES), F32),
            pltpu.VMEM(short_taps.shape, F32),
            pltpu.VMEM(rates.shape, F32),
            pltpu.VMEM(residues.shape, F32),
            pltpu.VMEM(tile, F32),
            pltpu.SMEM((block,), jnp.int32),
            pltpu.VMEM((GROUPS * 32, LANES), F32),
            pltpu.VMEM((9, *tile), F32),
            pltpu.VMEM((modes, *tile), F32),
            pltpu.VMEM((modes, *tile), F32),
            pltpu.VMEM((4, modes, *tile), F32),
            pltpu.VMEM((block, *tile), F32),
            pltpu.VMEM((block, *tile), F32),
            pltpu.VMEM((block, *tile), F32),
            pltpu.VMEM((GROUPS * pitch, LANES), F32),
            pltpu.VMEM((3, *twice), BF16),
            pltpu.VMEM((3, *twice), BF16),
            pltpu.VMEM((1, *twice), BF16),
            pltpu.VMEM((1, *twice), BF16),
            pltpu.VMEM((4, *twice), BF16),
            pltpu.VMEM((4, *twice), BF16),
            pltpu.VMEM((modes + 1, *tile), F32),
            pltpu.VMEM((ROW - 1, modes + 1, *tile), F32),
            pltpu.VMEM((modes + 1, *tile), F32),
            pltpu.VMEM((modes + 1, *tile), F32),
            pltpu.VMEM((REACH, modes + 1, *tile), F32),
            pltpu.VMEM((ROW - 1, modes, *tile), F32),
            pltpu.VMEM((modes, *tile), F32),
            dma((8,)),
            dma((2,)),
            dma((2,)),
            dma((2,)),
            dma((2,)),
            dma,
            dma((2,)),
            dma((REACH,)),
            dma((REACH,)),
            dma((2,)),
        ],
        compiler_params=pltpu.CompilerParams(
            collective_id=0, has_side_effects=True, vmem_limit_bytes=60 * 1024 * 1024
        ),
    )(
        query, keyed, valued, short_taps, rates, residues,
        skip_gain.reshape(tile), doc_ids,
    )


def solution(mesh):
    return jax.shard_map(
        functools.partial(on_device, mesh.shape["ctx"]),
        mesh=mesh,
        in_specs=(
            P("ctx", "tp"),
            P("ctx", "tp"),
            P("ctx", "tp"),
            P(None, None, "tp"),
            P(None, "tp"),
            P(None, "tp"),
            P("tp"),
            P("ctx"),
        ),
        out_specs=P("ctx", "tp"),
        check_vma=False,
    )
```

```python
import functools

import jax
import jax.numpy as jnp
from jax import lax
from jax.experimental import pallas as pl
from jax.experimental.pallas import tpu as pltpu
from jax.sharding import PartitionSpec as P

MESH = pl.DeviceIdType.MESH
F32 = jnp.float32
BF16 = jnp.bfloat16
ROW = 8
REACH = 4
LANES = 128
GROUPS = 8
STEP = 8
CHUNK = 64
SPLIT = 4


def tree_sum(terms):
    while len(terms) > 1:
        terms = [a + b for a, b in zip(terms[::2], terms[1::2])] + terms[len(terms) & ~1 :]
    return terms[0]


def flag(cond):
    return jnp.where(cond, 1.0, 0.0).astype(F32)


def kernel(
    n_ctx, pitch,
    q_hbm, k_hbm, v_hbm, taps_hbm, rates_hbm, resid_hbm, skip_hbm, ids_hbm,
    out,
    raw, xs, taps_in, rates_in, resid_in, skip_in, ids,
    prm, taps, rate, resid, power,
    gated, base, live_q, out_x,
    tail_out, tail_in, tail_q_out, tail_q_in, head_out, head_in,
    ends_out, ends_in, relay, relay_in, row_out, row_in, carry_out, carry_in,
    load_sem, tail_sems, tail_q_sems, head_sems, forward_sems, ends_sems,
    row_send, row_recv, carry_sems,
):
    block = q_hbm.shape[0]
    modes = rates_hbm.shape[0]
    last = block - 1
    me = lax.axis_index("ctx")
    tp = lax.axis_index("tp")
    y, z = me // ROW, lax.rem(me, ROW)
    n_rows = n_ctx // ROW
    root = y * ROW

    def at(device):
        return (device, tp)

    def remote(src, dst, send, recv, device):
        return pltpu.make_async_remote_copy(
            src_ref=src, dst_ref=dst, send_sem=send, recv_sem=recv,
            device_id=at(device), device_id_type=MESH,
        )

    barrier = pltpu.get_barrier_semaphore()

    def greet(device):
        pl.semaphore_signal(barrier, inc=1, device_id=at(device), device_id_type=MESH)

    @pl.when(z == 0)
    def _():
        for peer in range(1, ROW):
            greet(root + peer)
        for back in range(1, REACH + 1):
            @pl.when(y >= back)
            def _():
                greet(root - back * ROW)

    @pl.when(z == SPLIT - 1)
    def _():
        greet(me + 1)

    @pl.when(me > 0)
    def _():
        greet(me - 1)

    loads = [
        pltpu.make_async_copy(src, dst, load_sem.at[i])
        for i, (src, dst) in enumerate(
            [
                (k_hbm, raw.at[1]), (v_hbm, raw.at[2]), (ids_hbm, ids), (rates_hbm, rates_in),
                (taps_hbm, taps_in), (q_hbm, raw.at[0]), (resid_hbm, resid_in),
                (skip_hbm, skip_in),
            ]
        )
    ]
    for load in loads:
        load.start()

    def spread(s):
        for j in range(GROUPS):
            xs[s, pl.ds(j * pitch, block), :] = raw[s, :, j * LANES : (j + 1) * LANES].astype(F32)

    def token(s, t):
        return xs[s, pl.ds(t, GROUPS, stride=pitch), :]

    def splat(value):
        return jnp.full((GROUPS, LANES), value.astype(F32), F32)

    def put(ref, i, first, second):
        ref[i] = jnp.concatenate([first, second], axis=0).astype(BF16)

    def get(ref, i):
        both = ref[i].astype(F32)
        return both[:GROUPS], both[GROUPS:]

    loads[0].wait()
    spread(1)
    loads[1].wait()
    spread(2)
    loads[2].wait()
    id_0, id_1, id_end = splat(ids[0]), splat(ids[1]), splat(ids[last])
    for s in (1, 2):
        put(tail_out, s - 1, token(s, last - 1), token(s, last))
        put(head_out, s - 1, token(s, 0), token(s, 1))
    put(tail_out, 2, splat(ids[last - 1]), id_end)
    put(head_out, 2, id_0, id_1)
    put(head_out, 3, id_end, id_end)

    following = lax.rem(me + 1, n_ctx)
    tail = remote(tail_out, tail_in, tail_sems.at[0], tail_sems.at[1], following)
    tail_q = remote(tail_q_out, tail_q_in, tail_q_sems.at[0], tail_q_sems.at[1], following)

    def enter():
        rows_ahead = jnp.minimum(REACH, n_rows - 1 - y)
        expected = jnp.where(me < n_ctx - 1, 1, 0) + jnp.where(z == 0, rows_ahead, 1)
        pl.semaphore_wait(barrier, expected + jnp.where(z == SPLIT, 1, 0))

        @pl.when(me < n_ctx - 1)
        def _():
            tail.start()

    late = (z == 0) | (z == SPLIT - 1)

    @pl.when(jnp.logical_not(late))
    def _():
        enter()

    loads[3].wait()
    loads[4].wait()
    for j in range(GROUPS):
        cols = slice(j * LANES, (j + 1) * LANES)
        prm[pl.ds(j * 32, modes), :] = rates_in[:, cols]
        for s in range(3):
            for tap in range(3):
                prm[pl.ds(j * 32 + 16 + 3 * s + tap, 1), :] = taps_in[s, pl.ds(tap, 1), cols]
    for n in range(modes):
        rate[n] = prm[pl.ds(n, GROUPS, stride=32), :]
        power[0, n] = jnp.exp(-rate[n])
    for i in range(9):
        taps[i] = prm[pl.ds(16 + i, GROUPS, stride=32), :]

    def ends_step(i, carry):
        k1, k2, v1, v2, *state = carry
        decay = [power[0, n] for n in range(modes)]
        t0 = i * STEP
        for d in range(STEP):
            t = t0 + d
            here = ids[t]
            same1 = flag(here == ids[jnp.maximum(t - 1, 0)])
            same2 = flag(here == ids[jnp.maximum(t - 2, 0)])
            ends = flag((here == ids[last]) & (t >= 2))
            k0, v0 = token(1, t), token(2, t)
            kc = taps[3] * k0 + taps[4] * (k1 * same1) + taps[5] * (k2 * same2)
            vc = taps[6] * v0 + taps[7] * (v1 * same1) + taps[8] * (v2 * same2)
            g = (kc * vc).astype(BF16).astype(F32)
            gated[t] = g
            g = g * ends
            state = [decay[n] * state[n] + g for n in range(modes)]
            k1, k2, v1, v2 = k0, k1, v0, v1
        return (k1, k2, v1, v2, *state)

    zero = jnp.zeros((GROUPS, LANES), F32)
    _, _, _, _, *state = lax.fori_loop(0, block // STEP, ends_step, (zero,) * (4 + modes))
    for n in range(modes):
        ends_out[n] = state[n]
    ends_out[modes] = zero
    for i, steps in ((1, block - 2), (2, block), (3, ROW * block)):
        for n in range(modes):
            power[i, n] = jnp.exp(-rate[n] * float(steps))

    @pl.when(late)
    def _():
        enter()

    lifter = root + SPLIT - 1
    head = remote(head_out, head_in, head_sems.at[0], head_sems.at[1], lifter)
    forward = remote(relay, relay_in, forward_sems.at[0], forward_sems.at[1], root)
    slot = lax.rem(z + ROW - 1, ROW)
    ends = remote(ends_out, ends_in.at[slot], ends_sems.at[0], ends_sems.at[1], root)

    @pl.when(z == SPLIT)
    def _():
        head.start()
        ends.start()

    def first_two(s, before, x0, x1, before_ids, id0, id1):
        far, near = before
        id_far, id_near = before_ids
        a, b, c = taps[3 * s], taps[3 * s + 1], taps[3 * s + 2]
        return (
            a * x0 + b * (near * flag(id_near == id0)) + c * (far * flag(id_far == id0)),
            a * x1 + b * (x0 * flag(id0 == id1)) + c * (near * flag(id_near == id1)),
        )

    def first_gated(tail_ref, xk, xv, id0, id1):
        before_ids = get(tail_ref, 2)
        k = first_two(1, get(tail_ref, 0), *xk, before_ids, id0, id1)
        v = first_two(2, get(tail_ref, 1), *xv, before_ids, id0, id1)
        return [(a * b).astype(BF16).astype(F32) for a, b in zip(k, v)]

    def add_first(ref, g, id_near, id0, id1, end_id):
        joined, ending = flag(id0 == id1), flag(id1 == end_id)
        for n in range(modes):
            first = power[0, n] * (g[0] * joined) + g[1]
            ref[n] += power[1, n] * (first * ending)
        ref[modes] = flag(id_near == id0) * flag(id0 == end_id)

    def own_first():
        _, near_id = get(tail_in, 2)
        xk, xv = [(token(s, 0), token(s, 1)) for s in (1, 2)]
        gated[0], gated[1] = g = first_gated(tail_in, xk, xv, id_0, id_1)
        return g, near_id, id_0, id_1, id_end

    prompt = (z != 0) & (z != SPLIT)

    @pl.when(prompt)
    def _():
        tail.wait_recv()
        add_first(ends_out, *own_first())
        ends.start()

    loads[5].wait()
    spread(0)
    put(tail_q_out, 0, token(0, last - 1), token(0, last))

    @pl.when(me < n_ctx - 1)
    def _():
        tail_q.start()

    loads[6].wait()
    loads[7].wait()
    for j in range(GROUPS):
        prm[pl.ds(j * 32 + 8, modes), :] = resid_in[:, j * LANES : (j + 1) * LANES]
    for n in range(modes):
        resid[n] = prm[pl.ds(8 + n, GROUPS, stride=32), :]

    def local_step(i, carry):
        q1, q2, *state = carry
        decay = [power[0, n] for n in range(modes)]
        weight = [resid[n] for n in range(modes)]
        t0 = i * STEP
        for d in range(STEP):
            t = t0 + d
            here = ids[t]
            same1 = flag(here == ids[jnp.maximum(t - 1, 0)])
            same2 = flag(here == ids[jnp.maximum(t - 2, 0)])
            q0 = token(0, t)
            qc = taps[0] * q0 + taps[1] * (q1 * same1) + taps[2] * (q2 * same2)
            g = gated[t]
            if d < 2:
                g = g * flag(t >= 2)
            state = [decay[n] * (state[n] * same1) + g for n in range(modes)]
            long = tree_sum([weight[n] * state[n] for n in range(modes)])
            base[t] = qc * (long + skip_in[...] * g)
            live_q[t] = qc * flag(here == ids[1])
            q1, q2 = q0, q1
        return (q1, q2, *state)

    lax.fori_loop(0, block // STEP, local_step, (zero,) * (2 + modes))

    @pl.when((z == SPLIT) | ((z == 0) & (me > 0)))
    def _():
        tail.wait_recv()

    @pl.when(me == 0)
    def _():
        tail_in[...] = jnp.full(tail_in.shape, -1.0, BF16)
        tail_q_in[...] = jnp.zeros(tail_q_in.shape, BF16)

    @pl.when(z == 0)
    def _():
        add_first(ends_out, *own_first())

    @pl.when(z == SPLIT)
    def _():
        own_first()

    @pl.when(z == SPLIT - 1)
    def _():
        head.wait_recv()
        relay[...] = jnp.zeros(relay.shape, F32)
        (head_0, head_1), (head_end, _) = get(head_in, 2), get(head_in, 3)
        first = first_gated(tail_out, get(head_in, 0), get(head_in, 1), head_0, head_1)
        add_first(relay, first, id_end, head_0, head_1, head_end)
        forward.start()

    @pl.when(me > 0)
    def _():
        tail_q.wait_recv()

    def row_copy(back):
        return remote(
            row_out, row_in.at[back - 1], row_send.at[back - 1], row_recv.at[back - 1],
            lax.rem(me + back * ROW, n_ctx),
        )

    def carry_copy(peer):
        return remote(
            carry_out.at[peer - 1], carry_in, carry_sems.at[0], carry_sems.at[1], root + peer
        )

    def all_of(ref, sems):
        return remote(ref, ref, sems.at[0], sems.at[1], root)

    @pl.when(z == 0)
    def _():
        forward.wait_recv()
        all_of(ends_in, ends_sems).wait_recv()
        for n in range(modes + 1):
            ends_in[SPLIT - 1, n] += relay_in[n]
        hop = [power[2, n] for n in range(modes)]
        leap = [power[3, n] for n in range(modes)]
        total = [ends_out[n] for n in range(modes)]
        keep = ends_out[modes]
        for peer in range(1, ROW):
            k = ends_in[peer - 1, modes]
            keep = keep * k
            total = [total[n] * (hop[n] * k) + ends_in[peer - 1, n] for n in range(modes)]
        for n in range(modes):
            row_out[n] = total[n]
        row_out[modes] = keep

        orders = {0: (1, 2, 3, 4), 1: (1, 2, 4, 3), 2: (4, 1, 3, 2), 3: (4, 3, 2, 1)}
        for at_row in range(n_rows):
            @pl.when(y == at_row)
            def _():
                for back in orders.get(at_row, (3, 2, 1)):
                    if at_row + back < n_rows:
                        row_copy(back).start()

        carry_in[...] = jnp.zeros(carry_in.shape, F32)
        for back in range(REACH, 0, -1):
            @pl.when(y >= back)
            def _():
                row_copy(back).wait_recv()
                for n in range(modes):
                    carry_in[n] = (
                        leap[n] * row_in[back - 1, modes] * carry_in[n] + row_in[back - 1, n]
                    )

        now = [carry_in[n] for n in range(modes)]
        for peer in range(1, ROW):
            src = ends_out if peer == 1 else ends_in.at[peer - 2]
            k = src[modes]
            now = [now[n] * (hop[n] * k) + src[n] for n in range(modes)]
            for n in range(modes):
                carry_out[peer - 1, n] = now[n]
            carry_copy(peer).start()

    @pl.when(z > 0)
    def _():
        carry_copy(1).wait_recv()

    before_ids = get(tail_in, 2)
    q_first = first_two(0, get(tail_q_in, 0), token(0, 0), token(0, 1), before_ids, id_0, id_1)
    state = [carry_in[n] * flag(before_ids[1] == id_0) for n in range(modes)]
    for t in (0, 1):
        if t == 1:
            joined = flag(id_0 == id_1)
            state = [state[n] * joined for n in range(modes)]
        state = [power[0, n] * state[n] + gated[t] for n in range(modes)]
        long = tree_sum([resid[n] * state[n] for n in range(modes)])
        base[t] = q_first[t] * (long + skip_in[...] * gated[t])
        live_q[t] = zero

    def out_step(c, part):
        decay = [power[0, n] for n in range(modes)]
        for d in range(CHUNK):
            t = c * CHUNK + d
            part = [decay[n] * part[n] for n in range(modes)]
            out_x[pl.ds(t, GROUPS, stride=pitch), :] = base[t] + live_q[t] * tree_sum(list(part))
        for j in range(GROUPS):
            rows = pl.ds(pl.multiple_of(c * CHUNK, CHUNK), CHUNK)
            piece = out_x[pl.ds(j * pitch + pl.multiple_of(c * CHUNK, CHUNK), CHUNK), :]
            out[rows, j * LANES : (j + 1) * LANES] = piece.astype(BF16)
        return part

    lax.fori_loop(
        0, block // CHUNK, out_step, [resid[n] * jnp.exp(2.0 * rate[n]) * state[n] for n in range(modes)]
    )

    @pl.when(me < n_ctx - 1)
    def _():
        tail.wait_send()
        tail_q.wait_send()

    @pl.when(z == SPLIT - 1)
    def _():
        forward.wait_send()

    @pl.when(z == SPLIT)
    def _():
        head.wait_send()

    @pl.when(z > 0)
    def _():
        ends.wait_send()

    @pl.when(z == 0)
    def _():
        for back in range(1, REACH + 1):
            @pl.when(y + back < n_rows)
            def _():
                row_copy(back).wait_send()

        all_of(carry_out, carry_sems).wait_send()


def on_device(n_ctx, query, keyed, valued, short_taps, rates, residues, skip_gain, doc_ids):
    block, channels = query.shape
    modes = rates.shape[0]
    assert channels == GROUPS * LANES and block % CHUNK == 0 and modes == 8
    pitch = block + 8
    tile, twice = (GROUPS, LANES), (2 * GROUPS, LANES)
    dma = pltpu.SemaphoreType.DMA
    hbm = pl.BlockSpec(memory_space=pltpu.HBM)
    return pl.pallas_call(
        functools.partial(kernel, n_ctx, pitch),
        out_shape=pltpu.VMEM(query.shape, BF16),
        in_specs=[hbm] * 8,
        out_specs=pl.BlockSpec(memory_space=pltpu.VMEM),
        scratch_shapes=[
            pltpu.VMEM((3, block, channels), BF16),
            pltpu.VMEM((3, GROUPS * pitch, LANES), F32),
            pltpu.VMEM(short_taps.shape, F32),
            pltpu.VMEM(rates.shape, F32),
            pltpu.VMEM(residues.shape, F32),
            pltpu.VMEM(tile, F32),
            pltpu.SMEM((block,), jnp.int32),
            pltpu.VMEM((GROUPS * 32, LANES), F32),
            pltpu.VMEM((9, *tile), F32),
            pltpu.VMEM((modes, *tile), F32),
            pltpu.VMEM((modes, *tile), F32),
            pltpu.VMEM((4, modes, *tile), F32),
            pltpu.VMEM((block, *tile), F32),
            pltpu.VMEM((block, *tile), F32),
            pltpu.VMEM((block, *tile), F32),
            pltpu.VMEM((GROUPS * pitch, LANES), F32),
            pltpu.VMEM((3, *twice), BF16),
            pltpu.VMEM((3, *twice), BF16),
            pltpu.VMEM((1, *twice), BF16),
            pltpu.VMEM((1, *twice), BF16),
            pltpu.VMEM((4, *twice), BF16),
            pltpu.VMEM((4, *twice), BF16),
            pltpu.VMEM((modes + 1, *tile), F32),
            pltpu.VMEM((ROW - 1, modes + 1, *tile), F32),
            pltpu.VMEM((modes + 1, *tile), F32),
            pltpu.VMEM((modes + 1, *tile), F32),
            pltpu.VMEM((modes + 1, *tile), F32),
            pltpu.VMEM((REACH, modes + 1, *tile), F32),
            pltpu.VMEM((ROW - 1, modes, *tile), F32),
            pltpu.VMEM((modes, *tile), F32),
            dma((8,)),
            dma((2,)),
            dma((2,)),
            dma((2,)),
            dma((2,)),
            dma((2,)),
            dma((REACH,)),
            dma((REACH,)),
            dma((2,)),
        ],
        compiler_params=pltpu.CompilerParams(
            collective_id=0, has_side_effects=True, vmem_limit_bytes=60 * 1024 * 1024
        ),
    )(
        query, keyed, valued, short_taps, rates, residues,
        skip_gain.reshape(tile), doc_ids,
    )


def solution(mesh):
    return jax.shard_map(
        functools.partial(on_device, mesh.shape["ctx"]),
        mesh=mesh,
        in_specs=(
            P("ctx", "tp"),
            P("ctx", "tp"),
            P("ctx", "tp"),
            P(None, None, "tp"),
            P(None, "tp"),
            P(None, "tp"),
            P("tp"),
            P("ctx"),
        ),
        out_specs=P("ctx", "tp"),
        check_vma=False,
    )
```

```python
import functools

import jax
import jax.numpy as jnp
from jax import lax
from jax.experimental import pallas as pl
from jax.experimental.pallas import tpu as pltpu
from jax.sharding import PartitionSpec as P

MESH = pl.DeviceIdType.MESH
F32 = jnp.float32
BF16 = jnp.bfloat16
ROW = 8
REACH = 4
LANES = 128
GROUPS = 8
STEP = 8
CHUNK = 64
SPLIT = 4


def tree_sum(terms):
    while len(terms) > 1:
        terms = [a + b for a, b in zip(terms[::2], terms[1::2])] + terms[len(terms) & ~1 :]
    return terms[0]


def flag(cond):
    return jnp.where(cond, 1.0, 0.0).astype(F32)


def kernel(
    n_ctx, pitch,
    q_hbm, k_hbm, v_hbm, taps_hbm, rates_hbm, resid_hbm, skip_hbm, ids_hbm,
    out,
    raw, xs, taps_in, rates_in, resid_in, skip_in, ids,
    prm, taps, rate, resid, power,
    gated, base, live_q, out_x,
    tail_out, tail_in, tail_q_out, tail_q_in, head_out, head_in,
    ends_out, ends_in, relay, relay_in, row_out, row_in, carry_out, carry_in,
    load_sem, tail_sems, tail_q_sems, head_sems, forward_sems, ends_sems,
    row_send, row_recv, carry_sems,
):
    block = q_hbm.shape[0]
    modes = rates_hbm.shape[0]
    last = block - 1
    me = lax.axis_index("ctx")
    tp = lax.axis_index("tp")
    y, z = me // ROW, lax.rem(me, ROW)
    n_rows = n_ctx // ROW
    root = y * ROW

    def at(device):
        return (device, tp)

    def remote(src, dst, send, recv, device):
        return pltpu.make_async_remote_copy(
            src_ref=src, dst_ref=dst, send_sem=send, recv_sem=recv,
            device_id=at(device), device_id_type=MESH,
        )

    barrier = pltpu.get_barrier_semaphore()

    def greet(device):
        pl.semaphore_signal(barrier, inc=1, device_id=at(device), device_id_type=MESH)

    @pl.when(z == 0)
    def _():
        for peer in range(1, ROW):
            greet(root + peer)
        for back in range(1, REACH + 1):
            @pl.when(y >= back)
            def _():
                greet(root - back * ROW)

    @pl.when(z == SPLIT - 1)
    def _():
        greet(me + 1)

    @pl.when(me > 0)
    def _():
        greet(me - 1)

    loads = [
        pltpu.make_async_copy(src, dst, load_sem.at[i])
        for i, (src, dst) in enumerate(
            [
                (k_hbm, raw.at[1]), (v_hbm, raw.at[2]), (ids_hbm, ids), (rates_hbm, rates_in),
                (taps_hbm, taps_in), (q_hbm, raw.at[0]), (resid_hbm, resid_in),
                (skip_hbm, skip_in),
            ]
        )
    ]
    for load in loads:
        load.start()

    def spread(s):
        for j in range(GROUPS):
            xs[s, pl.ds(j * pitch, block), :] = raw[s, :, j * LANES : (j + 1) * LANES].astype(F32)

    def token(s, t):
        return xs[s, pl.ds(t, GROUPS, stride=pitch), :]

    def splat(value):
        return jnp.full((GROUPS, LANES), value.astype(F32), F32)

    def put(ref, i, first, second):
        ref[i] = jnp.concatenate([first, second], axis=0).astype(BF16)

    def get(ref, i):
        both = ref[i].astype(F32)
        return both[:GROUPS], both[GROUPS:]

    loads[0].wait()
    spread(1)
    loads[1].wait()
    spread(2)
    loads[2].wait()
    id_0, id_1, id_end = splat(ids[0]), splat(ids[1]), splat(ids[last])
    for s in (1, 2):
        put(tail_out, s - 1, token(s, last - 1), token(s, last))
        put(head_out, s - 1, token(s, 0), token(s, 1))
    put(tail_out, 2, splat(ids[last - 1]), id_end)
    put(head_out, 2, id_0, id_1)
    put(head_out, 3, id_end, id_end)

    following = lax.rem(me + 1, n_ctx)
    tail = remote(tail_out, tail_in, tail_sems.at[0], tail_sems.at[1], following)
    tail_q = remote(tail_q_out, tail_q_in, tail_q_sems.at[0], tail_q_sems.at[1], following)

    def enter():
        rows_ahead = jnp.minimum(REACH, n_rows - 1 - y)
        expected = jnp.where(me < n_ctx - 1, 1, 0) + jnp.where(z == 0, rows_ahead, 1)
        pl.semaphore_wait(barrier, expected + jnp.where(z == SPLIT, 1, 0))

        @pl.when(me < n_ctx - 1)
        def _():
            tail.start()

    late = (z == 0) | (z == SPLIT - 1)

    @pl.when(jnp.logical_not(late))
    def _():
        enter()

    loads[3].wait()
    loads[4].wait()
    for j in range(GROUPS):
        cols = slice(j * LANES, (j + 1) * LANES)
        prm[pl.ds(j * 32, modes), :] = rates_in[:, cols]
        for s in range(3):
            for tap in range(3):
                prm[pl.ds(j * 32 + 16 + 3 * s + tap, 1), :] = taps_in[s, pl.ds(tap, 1), cols]
    for n in range(modes):
        rate[n] = prm[pl.ds(n, GROUPS, stride=32), :]
        power[0, n] = jnp.exp(-rate[n])
    for i in range(9):
        taps[i] = prm[pl.ds(16 + i, GROUPS, stride=32), :]

    def ends_step(i, carry):
        k1, k2, v1, v2, *state = carry
        decay = [power[0, n] for n in range(modes)]
        t0 = i * STEP
        for d in range(STEP):
            t = t0 + d
            here = ids[t]
            same1 = flag(here == ids[jnp.maximum(t - 1, 0)])
            same2 = flag(here == ids[jnp.maximum(t - 2, 0)])
            ends = flag((here == ids[last]) & (t >= 2))
            k0, v0 = token(1, t), token(2, t)
            kc = taps[3] * k0 + taps[4] * (k1 * same1) + taps[5] * (k2 * same2)
            vc = taps[6] * v0 + taps[7] * (v1 * same1) + taps[8] * (v2 * same2)
            g = (kc * vc).astype(BF16).astype(F32)
            gated[t] = g
            g = g * ends
            state = [decay[n] * state[n] + g for n in range(modes)]
            k1, k2, v1, v2 = k0, k1, v0, v1
        return (k1, k2, v1, v2, *state)

    zero = jnp.zeros((GROUPS, LANES), F32)
    _, _, _, _, *state = lax.fori_loop(0, block // STEP, ends_step, (zero,) * (4 + modes))
    for n in range(modes):
        ends_out[n] = state[n]
    ends_out[modes] = zero
    for i, steps in ((1, block - 2), (2, block), (3, ROW * block)):
        for n in range(modes):
            power[i, n] = jnp.exp(-rate[n] * float(steps))

    @pl.when(late)
    def _():
        enter()

    lifter = root + SPLIT - 1
    head = remote(head_out, head_in, head_sems.at[0], head_sems.at[1], lifter)
    forward = remote(relay, relay_in, forward_sems.at[0], forward_sems.at[1], root)
    slot = lax.rem(z + ROW - 1, ROW)
    ends = remote(ends_out, ends_in.at[slot], ends_sems.at[0], ends_sems.at[1], root)

    @pl.when(z == SPLIT)
    def _():
        head.start()
        ends.start()

    def first_two(s, before, x0, x1, before_ids, id0, id1):
        far, near = before
        id_far, id_near = before_ids
        a, b, c = taps[3 * s], taps[3 * s + 1], taps[3 * s + 2]
        return (
            a * x0 + b * (near * flag(id_near == id0)) + c * (far * flag(id_far == id0)),
            a * x1 + b * (x0 * flag(id0 == id1)) + c * (near * flag(id_near == id1)),
        )

    def first_gated(tail_ref, xk, xv, id0, id1):
        before_ids = get(tail_ref, 2)
        k = first_two(1, get(tail_ref, 0), *xk, before_ids, id0, id1)
        v = first_two(2, get(tail_ref, 1), *xv, before_ids, id0, id1)
        return [(a * b).astype(BF16).astype(F32) for a, b in zip(k, v)]

    def add_first(ref, g, id_near, id0, id1, end_id):
        joined, ending = flag(id0 == id1), flag(id1 == end_id)
        for n in range(modes):
            first = power[0, n] * (g[0] * joined) + g[1]
            ref[n] += power[1, n] * (first * ending)
        ref[modes] = flag(id_near == id0) * flag(id0 == end_id)

    def own_first():
        _, near_id = get(tail_in, 2)
        xk, xv = [(token(s, 0), token(s, 1)) for s in (1, 2)]
        gated[0], gated[1] = g = first_gated(tail_in, xk, xv, id_0, id_1)
        return g, near_id, id_0, id_1, id_end

    prompt = (z != 0) & (z != SPLIT)

    @pl.when(prompt)
    def _():
        tail.wait_recv()
        add_first(ends_out, *own_first())
        ends.start()

    loads[5].wait()
    spread(0)
    put(tail_q_out, 0, token(0, last - 1), token(0, last))

    @pl.when(me < n_ctx - 1)
    def _():
        tail_q.start()

    loads[6].wait()
    loads[7].wait()
    for j in range(GROUPS):
        prm[pl.ds(j * 32 + 8, modes), :] = resid_in[:, j * LANES : (j + 1) * LANES]
    for n in range(modes):
        resid[n] = prm[pl.ds(8 + n, GROUPS, stride=32), :]

    def local_step(i, carry):
        q1, q2, *state = carry
        decay = [power[0, n] for n in range(modes)]
        weight = [resid[n] for n in range(modes)]
        t0 = i * STEP
        for d in range(STEP):
            t = t0 + d
            here = ids[t]
            same1 = flag(here == ids[jnp.maximum(t - 1, 0)])
            same2 = flag(here == ids[jnp.maximum(t - 2, 0)])
            q0 = token(0, t)
            qc = taps[0] * q0 + taps[1] * (q1 * same1) + taps[2] * (q2 * same2)
            g = gated[t]
            if d < 2:
                g = g * flag(t >= 2)
            state = [decay[n] * (state[n] * same1) + g for n in range(modes)]
            long = tree_sum([weight[n] * state[n] for n in range(modes)])
            base[t] = qc * (long + skip_in[...] * g)
            live_q[t] = qc * flag(here == ids[1])
            q1, q2 = q0, q1
        return (q1, q2, *state)

    lax.fori_loop(0, block // STEP, local_step, (zero,) * (2 + modes))

    @pl.when((z == SPLIT) | ((z == 0) & (me > 0)))
    def _():
        tail.wait_recv()

    @pl.when(me == 0)
    def _():
        tail_in[...] = jnp.full(tail_in.shape, -1.0, BF16)
        tail_q_in[...] = jnp.zeros(tail_q_in.shape, BF16)

    @pl.when(z == 0)
    def _():
        add_first(ends_out, *own_first())

    @pl.when(z == SPLIT)
    def _():
        own_first()

    @pl.when(z == SPLIT - 1)
    def _():
        head.wait_recv()
        relay[...] = jnp.zeros(relay.shape, F32)
        (head_0, head_1), (head_end, _) = get(head_in, 2), get(head_in, 3)
        first = first_gated(tail_out, get(head_in, 0), get(head_in, 1), head_0, head_1)
        add_first(relay, first, id_end, head_0, head_1, head_end)
        forward.start()

    @pl.when(me > 0)
    def _():
        tail_q.wait_recv()

    def row_copy(back):
        return remote(
            row_out.at[pl.ds(0, modes + (back < REACH))],
            row_in.at[back - 1, pl.ds(0, modes + (back < REACH))],
            row_send.at[back - 1], row_recv.at[back - 1],
            lax.rem(me + back * ROW, n_ctx),
        )

    def carry_copy(peer):
        return remote(
            carry_out.at[peer - 1], carry_in, carry_sems.at[0], carry_sems.at[1], root + peer
        )

    def all_of(ref, sems):
        return remote(ref, ref, sems.at[0], sems.at[1], root)

    @pl.when(z == 0)
    def _():
        forward.wait_recv()
        all_of(ends_in, ends_sems).wait_recv()
        for n in range(modes + 1):
            ends_in[SPLIT - 1, n] += relay_in[n]
        hop = [power[2, n] for n in range(modes)]
        leap = [power[3, n] for n in range(modes)]
        total = [ends_out[n] for n in range(modes)]
        keep = ends_out[modes]
        for peer in range(1, ROW):
            k = ends_in[peer - 1, modes]
            keep = keep * k
            total = [total[n] * (hop[n] * k) + ends_in[peer - 1, n] for n in range(modes)]
        for n in range(modes):
            row_out[n] = total[n]
        row_out[modes] = keep

        orders = {0: (1, 2, 3, 4), 1: (1, 2, 4, 3), 2: (4, 1, 3, 2), 3: (4, 3, 2, 1)}
        for at_row in range(n_rows):
            @pl.when(y == at_row)
            def _():
                for back in orders.get(at_row, (3, 2, 1)):
                    if at_row + back < n_rows:
                        row_copy(back).start()

        carry_in[...] = jnp.zeros(carry_in.shape, F32)
        for back in range(REACH, 0, -1):
            @pl.when(y >= back)
            def _():
                row_copy(back).wait_recv()
                for n in range(modes):
                    if back == REACH:
                        carry_in[n] = row_in[back - 1, n]
                    else:
                        carry_in[n] = (
                            leap[n] * row_in[back - 1, modes] * carry_in[n] + row_in[back - 1, n]
                        )

        now = [carry_in[n] for n in range(modes)]
        for peer in range(1, ROW):
            src = ends_out if peer == 1 else ends_in.at[peer - 2]
            k = src[modes]
            now = [now[n] * (hop[n] * k) + src[n] for n in range(modes)]
            for n in range(modes):
                carry_out[peer - 1, n] = now[n]
            carry_copy(peer).start()

    @pl.when(z > 0)
    def _():
        carry_copy(1).wait_recv()

    before_ids = get(tail_in, 2)
    q_first = first_two(0, get(tail_q_in, 0), token(0, 0), token(0, 1), before_ids, id_0, id_1)
    state = [carry_in[n] * flag(before_ids[1] == id_0) for n in range(modes)]
    for t in (0, 1):
        if t == 1:
            joined = flag(id_0 == id_1)
            state = [state[n] * joined for n in range(modes)]
        state = [power[0, n] * state[n] + gated[t] for n in range(modes)]
        long = tree_sum([resid[n] * state[n] for n in range(modes)])
        base[t] = q_first[t] * (long + skip_in[...] * gated[t])
        live_q[t] = zero

    def out_step(c, part):
        decay = [power[0, n] for n in range(modes)]
        for d in range(CHUNK):
            t = c * CHUNK + d
            part = [decay[n] * part[n] for n in range(modes)]
            out_x[pl.ds(t, GROUPS, stride=pitch), :] = base[t] + live_q[t] * tree_sum(list(part))
        for j in range(GROUPS):
            rows = pl.ds(pl.multiple_of(c * CHUNK, CHUNK), CHUNK)
            piece = out_x[pl.ds(j * pitch + pl.multiple_of(c * CHUNK, CHUNK), CHUNK), :]
            out[rows, j * LANES : (j + 1) * LANES] = piece.astype(BF16)
        return part

    lax.fori_loop(
        0, block // CHUNK, out_step, [resid[n] * jnp.exp(2.0 * rate[n]) * state[n] for n in range(modes)]
    )

    @pl.when(me < n_ctx - 1)
    def _():
        tail.wait_send()
        tail_q.wait_send()

    @pl.when(z == SPLIT - 1)
    def _():
        forward.wait_send()

    @pl.when(z == SPLIT)
    def _():
        head.wait_send()

    @pl.when(z > 0)
    def _():
        ends.wait_send()

    @pl.when(z == 0)
    def _():
        for back in range(1, REACH + 1):
            @pl.when(y + back < n_rows)
            def _():
                row_copy(back).wait_send()

        all_of(carry_out, carry_sems).wait_send()


def on_device(n_ctx, query, keyed, valued, short_taps, rates, residues, skip_gain, doc_ids):
    block, channels = query.shape
    modes = rates.shape[0]
    assert channels == GROUPS * LANES and block % CHUNK == 0 and modes == 8
    pitch = block + 8
    tile, twice = (GROUPS, LANES), (2 * GROUPS, LANES)
    dma = pltpu.SemaphoreType.DMA
    hbm = pl.BlockSpec(memory_space=pltpu.HBM)
    return pl.pallas_call(
        functools.partial(kernel, n_ctx, pitch),
        out_shape=pltpu.VMEM(query.shape, BF16),
        in_specs=[hbm] * 8,
        out_specs=pl.BlockSpec(memory_space=pltpu.VMEM),
        scratch_shapes=[
            pltpu.VMEM((3, block, channels), BF16),
            pltpu.VMEM((3, GROUPS * pitch, LANES), F32),
            pltpu.VMEM(short_taps.shape, F32),
            pltpu.VMEM(rates.shape, F32),
            pltpu.VMEM(residues.shape, F32),
            pltpu.VMEM(tile, F32),
            pltpu.SMEM((block,), jnp.int32),
            pltpu.VMEM((GROUPS * 32, LANES), F32),
            pltpu.VMEM((9, *tile), F32),
            pltpu.VMEM((modes, *tile), F32),
            pltpu.VMEM((modes, *tile), F32),
            pltpu.VMEM((4, modes, *tile), F32),
            pltpu.VMEM((block, *tile), F32),
            pltpu.VMEM((block, *tile), F32),
            pltpu.VMEM((block, *tile), F32),
            pltpu.VMEM((GROUPS * pitch, LANES), F32),
            pltpu.VMEM((3, *twice), BF16),
            pltpu.VMEM((3, *twice), BF16),
            pltpu.VMEM((1, *twice), BF16),
            pltpu.VMEM((1, *twice), BF16),
            pltpu.VMEM((4, *twice), BF16),
            pltpu.VMEM((4, *twice), BF16),
            pltpu.VMEM((modes + 1, *tile), F32),
            pltpu.VMEM((ROW - 1, modes + 1, *tile), F32),
            pltpu.VMEM((modes + 1, *tile), F32),
            pltpu.VMEM((modes + 1, *tile), F32),
            pltpu.VMEM((modes + 1, *tile), F32),
            pltpu.VMEM((REACH, modes + 1, *tile), F32),
            pltpu.VMEM((ROW - 1, modes, *tile), F32),
            pltpu.VMEM((modes, *tile), F32),
            dma((8,)),
            dma((2,)),
            dma((2,)),
            dma((2,)),
            dma((2,)),
            dma((2,)),
            dma((REACH,)),
            dma((REACH,)),
            dma((2,)),
        ],
        compiler_params=pltpu.CompilerParams(
            collective_id=0, has_side_effects=True, vmem_limit_bytes=60 * 1024 * 1024
        ),
    )(
        query, keyed, valued, short_taps, rates, residues,
        skip_gain.reshape(tile), doc_ids,
    )


def solution(mesh):
    return jax.shard_map(
        functools.partial(on_device, mesh.shape["ctx"]),
        mesh=mesh,
        in_specs=(
            P("ctx", "tp"),
            P("ctx", "tp"),
            P("ctx", "tp"),
            P(None, None, "tp"),
            P(None, "tp"),
            P(None, "tp"),
            P("tp"),
            P("ctx"),
        ),
        out_specs=P("ctx", "tp"),
        check_vma=False,
    )
```

```python
import functools

import jax
import jax.numpy as jnp
from jax import lax
from jax.experimental import pallas as pl
from jax.experimental.pallas import tpu as pltpu
from jax.sharding import PartitionSpec as P

MESH = pl.DeviceIdType.MESH
F32 = jnp.float32
BF16 = jnp.bfloat16
ROW = 8
REACH = 4
LANES = 128
GROUPS = 8
STEP = 16
CHUNK = 128
SPLIT = 4


def tree_sum(terms):
    while len(terms) > 1:
        terms = [a + b for a, b in zip(terms[::2], terms[1::2])] + terms[len(terms) & ~1 :]
    return terms[0]


def flag(cond):
    return jnp.where(cond, 1.0, 0.0).astype(F32)


def kernel(
    n_ctx, pitch,
    q_hbm, k_hbm, v_hbm, taps_hbm, rates_hbm, resid_hbm, skip_hbm, ids_hbm,
    out,
    raw, xs, taps_in, rates_in, resid_in, skip_in, ids,
    prm, taps, rate, resid, power,
    gated, base, live_q, out_x,
    tail_out, tail_in, tail_q_out, tail_q_in, head_out, head_in,
    ends_out, ends_in, relay, relay_in, row_out, row_in, carry_out, carry_in,
    load_sem, tail_sems, tail_q_sems, head_sems, forward_sems, ends_sems,
    row_send, row_recv, carry_sems,
):
    block = q_hbm.shape[0]
    modes = rates_hbm.shape[0]
    last = block - 1
    me = lax.axis_index("ctx")
    tp = lax.axis_index("tp")
    y, z = me // ROW, lax.rem(me, ROW)
    n_rows = n_ctx // ROW
    root = y * ROW

    def at(device):
        return (device, tp)

    def remote(src, dst, send, recv, device):
        return pltpu.make_async_remote_copy(
            src_ref=src, dst_ref=dst, send_sem=send, recv_sem=recv,
            device_id=at(device), device_id_type=MESH,
        )

    barrier = pltpu.get_barrier_semaphore()

    def greet(device):
        pl.semaphore_signal(barrier, inc=1, device_id=at(device), device_id_type=MESH)

    @pl.when(z == 0)
    def _():
        for peer in range(1, ROW):
            greet(root + peer)
        for back in range(1, REACH + 1):
            @pl.when(y >= back)
            def _():
                greet(root - back * ROW)

    @pl.when(z == SPLIT - 1)
    def _():
        greet(me + 1)

    @pl.when(me > 0)
    def _():
        greet(me - 1)

    loads = [
        pltpu.make_async_copy(src, dst, load_sem.at[i])
        for i, (src, dst) in enumerate(
            [
                (k_hbm, raw.at[1]), (v_hbm, raw.at[2]), (ids_hbm, ids), (rates_hbm, rates_in),
                (taps_hbm, taps_in), (q_hbm, raw.at[0]), (resid_hbm, resid_in),
                (skip_hbm, skip_in),
            ]
        )
    ]
    for load in loads:
        load.start()

    def spread(s):
        for j in range(GROUPS):
            xs[s, pl.ds(j * pitch, block), :] = raw[s, :, j * LANES : (j + 1) * LANES].astype(F32)

    def token(s, t):
        return xs[s, pl.ds(t, GROUPS, stride=pitch), :]

    def splat(value):
        return jnp.full((GROUPS, LANES), value.astype(F32), F32)

    def put(ref, i, first, second):
        ref[i] = jnp.concatenate([first, second], axis=0).astype(BF16)

    def get(ref, i):
        both = ref[i].astype(F32)
        return both[:GROUPS], both[GROUPS:]

    loads[0].wait()
    spread(1)
    loads[1].wait()
    spread(2)
    loads[2].wait()
    id_0, id_1, id_end = splat(ids[0]), splat(ids[1]), splat(ids[last])
    for s in (1, 2):
        put(tail_out, s - 1, token(s, last - 1), token(s, last))
        put(head_out, s - 1, token(s, 0), token(s, 1))
    put(tail_out, 2, splat(ids[last - 1]), id_end)
    put(head_out, 2, id_0, id_1)
    put(head_out, 3, id_end, id_end)

    following = lax.rem(me + 1, n_ctx)
    tail = remote(tail_out, tail_in, tail_sems.at[0], tail_sems.at[1], following)
    tail_q = remote(tail_q_out, tail_q_in, tail_q_sems.at[0], tail_q_sems.at[1], following)

    def enter():
        rows_ahead = jnp.minimum(REACH, n_rows - 1 - y)
        expected = jnp.where(me < n_ctx - 1, 1, 0) + jnp.where(z == 0, rows_ahead, 1)
        pl.semaphore_wait(barrier, expected + jnp.where(z == SPLIT, 1, 0))

        @pl.when(me < n_ctx - 1)
        def _():
            tail.start()

    late = (z == 0) | (z == SPLIT - 1)

    @pl.when(jnp.logical_not(late))
    def _():
        enter()

    loads[3].wait()
    loads[4].wait()
    for j in range(GROUPS):
        cols = slice(j * LANES, (j + 1) * LANES)
        prm[pl.ds(j * 32, modes), :] = rates_in[:, cols]
        for s in range(3):
            for tap in range(3):
                prm[pl.ds(j * 32 + 16 + 3 * s + tap, 1), :] = taps_in[s, pl.ds(tap, 1), cols]
    for n in range(modes):
        rate[n] = prm[pl.ds(n, GROUPS, stride=32), :]
        power[0, n] = jnp.exp(-rate[n])
    for i in range(9):
        taps[i] = prm[pl.ds(16 + i, GROUPS, stride=32), :]

    def ends_step(i, carry):
        k1, k2, v1, v2, *state = carry
        decay = [power[0, n] for n in range(modes)]
        t0 = i * STEP
        for d in range(STEP):
            t = t0 + d
            here = ids[t]
            same1 = flag(here == ids[jnp.maximum(t - 1, 0)])
            same2 = flag(here == ids[jnp.maximum(t - 2, 0)])
            ends = flag((here == ids[last]) & (t >= 2))
            k0, v0 = token(1, t), token(2, t)
            kc = taps[3] * k0 + taps[4] * (k1 * same1) + taps[5] * (k2 * same2)
            vc = taps[6] * v0 + taps[7] * (v1 * same1) + taps[8] * (v2 * same2)
            g = (kc * vc).astype(BF16).astype(F32)
            gated[t] = g
            g = g * ends
            state = [decay[n] * state[n] + g for n in range(modes)]
            k1, k2, v1, v2 = k0, k1, v0, v1
        return (k1, k2, v1, v2, *state)

    zero = jnp.zeros((GROUPS, LANES), F32)
    _, _, _, _, *state = lax.fori_loop(0, block // STEP, ends_step, (zero,) * (4 + modes))
    for n in range(modes):
        ends_out[n] = state[n]
    ends_out[modes] = zero
    for i, steps in ((1, block - 2), (2, block), (3, ROW * block)):
        for n in range(modes):
            power[i, n] = jnp.exp(-rate[n] * float(steps))

    @pl.when(late)
    def _():
        enter()

    lifter = root + SPLIT - 1
    head = remote(head_out, head_in, head_sems.at[0], head_sems.at[1], lifter)
    forward = remote(relay, relay_in, forward_sems.at[0], forward_sems.at[1], root)
    slot = lax.rem(z + ROW - 1, ROW)
    ends = remote(ends_out, ends_in.at[slot], ends_sems.at[0], ends_sems.at[1], root)

    @pl.when(z == SPLIT)
    def _():
        head.start()
        ends.start()

    def first_two(s, before, x0, x1, before_ids, id0, id1):
        far, near = before
        id_far, id_near = before_ids
        a, b, c = taps[3 * s], taps[3 * s + 1], taps[3 * s + 2]
        return (
            a * x0 + b * (near * flag(id_near == id0)) + c * (far * flag(id_far == id0)),
            a * x1 + b * (x0 * flag(id0 == id1)) + c * (near * flag(id_near == id1)),
        )

    def first_gated(tail_ref, xk, xv, id0, id1):
        before_ids = get(tail_ref, 2)
        k = first_two(1, get(tail_ref, 0), *xk, before_ids, id0, id1)
        v = first_two(2, get(tail_ref, 1), *xv, before_ids, id0, id1)
        return [(a * b).astype(BF16).astype(F32) for a, b in zip(k, v)]

    def add_first(ref, g, id_near, id0, id1, end_id):
        joined, ending = flag(id0 == id1), flag(id1 == end_id)
        for n in range(modes):
            first = power[0, n] * (g[0] * joined) + g[1]
            ref[n] += power[1, n] * (first * ending)
        ref[modes] = flag(id_near == id0) * flag(id0 == end_id)

    def own_first():
        _, near_id = get(tail_in, 2)
        xk, xv = [(token(s, 0), token(s, 1)) for s in (1, 2)]
        gated[0], gated[1] = g = first_gated(tail_in, xk, xv, id_0, id_1)
        return g, near_id, id_0, id_1, id_end

    prompt = (z != 0) & (z != SPLIT)

    @pl.when(prompt)
    def _():
        tail.wait_recv()
        add_first(ends_out, *own_first())
        ends.start()

    loads[5].wait()
    spread(0)
    put(tail_q_out, 0, token(0, last - 1), token(0, last))

    @pl.when(me < n_ctx - 1)
    def _():
        tail_q.start()

    loads[6].wait()
    loads[7].wait()
    for j in range(GROUPS):
        prm[pl.ds(j * 32 + 8, modes), :] = resid_in[:, j * LANES : (j + 1) * LANES]
    for n in range(modes):
        resid[n] = prm[pl.ds(8 + n, GROUPS, stride=32), :]

    def local_step(i, carry):
        q1, q2, *state = carry
        decay = [power[0, n] for n in range(modes)]
        weight = [resid[n] for n in range(modes)]
        t0 = i * STEP
        for d in range(STEP):
            t = t0 + d
            here = ids[t]
            same1 = flag(here == ids[jnp.maximum(t - 1, 0)])
            same2 = flag(here == ids[jnp.maximum(t - 2, 0)])
            q0 = token(0, t)
            qc = taps[0] * q0 + taps[1] * (q1 * same1) + taps[2] * (q2 * same2)
            g = gated[t]
            if d < 2:
                g = g * flag(t >= 2)
            state = [decay[n] * (state[n] * same1) + g for n in range(modes)]
            long = tree_sum([weight[n] * state[n] for n in range(modes)])
            base[t] = qc * (long + skip_in[...] * g)
            live_q[t] = qc * flag(here == ids[1])
            q1, q2 = q0, q1
        return (q1, q2, *state)

    lax.fori_loop(0, block // STEP, local_step, (zero,) * (2 + modes))

    @pl.when((z == SPLIT) | ((z == 0) & (me > 0)))
    def _():
        tail.wait_recv()

    @pl.when(me == 0)
    def _():
        tail_in[...] = jnp.full(tail_in.shape, -1.0, BF16)
        tail_q_in[...] = jnp.zeros(tail_q_in.shape, BF16)

    @pl.when(z == 0)
    def _():
        add_first(ends_out, *own_first())

    @pl.when(z == SPLIT)
    def _():
        own_first()

    @pl.when(z == SPLIT - 1)
    def _():
        head.wait_recv()
        relay[...] = jnp.zeros(relay.shape, F32)
        (head_0, head_1), (head_end, _) = get(head_in, 2), get(head_in, 3)
        first = first_gated(tail_out, get(head_in, 0), get(head_in, 1), head_0, head_1)
        add_first(relay, first, id_end, head_0, head_1, head_end)
        forward.start()

    @pl.when(me > 0)
    def _():
        tail_q.wait_recv()

    def row_copy(back):
        return remote(
            row_out.at[pl.ds(0, modes + (back < REACH))],
            row_in.at[back - 1, pl.ds(0, modes + (back < REACH))],
            row_send.at[back - 1], row_recv.at[back - 1],
            lax.rem(me + back * ROW, n_ctx),
        )

    def carry_copy(peer):
        return remote(
            carry_out.at[peer - 1], carry_in, carry_sems.at[0], carry_sems.at[1], root + peer
        )

    def all_of(ref, sems):
        return remote(ref, ref, sems.at[0], sems.at[1], root)

    @pl.when(z == 0)
    def _():
        forward.wait_recv()
        all_of(ends_in, ends_sems).wait_recv()
        for n in range(modes + 1):
            ends_in[SPLIT - 1, n] += relay_in[n]
        hop = [power[2, n] for n in range(modes)]
        leap = [power[3, n] for n in range(modes)]
        total = [ends_out[n] for n in range(modes)]
        keep = ends_out[modes]
        for peer in range(1, ROW):
            k = ends_in[peer - 1, modes]
            keep = keep * k
            total = [total[n] * (hop[n] * k) + ends_in[peer - 1, n] for n in range(modes)]
        for n in range(modes):
            row_out[n] = total[n]
        row_out[modes] = keep

        orders = {0: (1, 2, 3, 4), 1: (1, 2, 4, 3), 2: (4, 1, 3, 2), 3: (4, 3, 2, 1)}
        for at_row in range(n_rows):
            @pl.when(y == at_row)
            def _():
                for back in orders.get(at_row, (3, 2, 1)):
                    if at_row + back < n_rows:
                        row_copy(back).start()

        carry_in[...] = jnp.zeros(carry_in.shape, F32)
        for back in range(REACH, 0, -1):
            @pl.when(y >= back)
            def _():
                row_copy(back).wait_recv()
                for n in range(modes):
                    if back == REACH:
                        carry_in[n] = row_in[back - 1, n]
                    else:
                        carry_in[n] = (
                            leap[n] * row_in[back - 1, modes] * carry_in[n] + row_in[back - 1, n]
                        )

        now = [carry_in[n] for n in range(modes)]
        for peer in range(1, ROW):
            src = ends_out if peer == 1 else ends_in.at[peer - 2]
            k = src[modes]
            now = [now[n] * (hop[n] * k) + src[n] for n in range(modes)]
            for n in range(modes):
                carry_out[peer - 1, n] = now[n]
            carry_copy(peer).start()

    @pl.when(z > 0)
    def _():
        carry_copy(1).wait_recv()

    before_ids = get(tail_in, 2)
    q_first = first_two(0, get(tail_q_in, 0), token(0, 0), token(0, 1), before_ids, id_0, id_1)
    state = [carry_in[n] * flag(before_ids[1] == id_0) for n in range(modes)]
    for t in (0, 1):
        if t == 1:
            joined = flag(id_0 == id_1)
            state = [state[n] * joined for n in range(modes)]
        state = [power[0, n] * state[n] + gated[t] for n in range(modes)]
        long = tree_sum([resid[n] * state[n] for n in range(modes)])
        base[t] = q_first[t] * (long + skip_in[...] * gated[t])
        live_q[t] = zero

    def out_step(c, part):
        decay = [power[0, n] for n in range(modes)]
        for d in range(CHUNK):
            t = c * CHUNK + d
            part = [decay[n] * part[n] for n in range(modes)]
            out_x[pl.ds(t, GROUPS, stride=pitch), :] = base[t] + live_q[t] * tree_sum(list(part))
        for j in range(GROUPS):
            rows = pl.ds(pl.multiple_of(c * CHUNK, CHUNK), CHUNK)
            piece = out_x[pl.ds(j * pitch + pl.multiple_of(c * CHUNK, CHUNK), CHUNK), :]
            out[rows, j * LANES : (j + 1) * LANES] = piece.astype(BF16)
        return part

    lax.fori_loop(
        0, block // CHUNK, out_step, [resid[n] * jnp.exp(2.0 * rate[n]) * state[n] for n in range(modes)]
    )

    @pl.when(me < n_ctx - 1)
    def _():
        tail.wait_send()
        tail_q.wait_send()

    @pl.when(z == SPLIT - 1)
    def _():
        forward.wait_send()

    @pl.when(z == SPLIT)
    def _():
        head.wait_send()

    @pl.when(z > 0)
    def _():
        ends.wait_send()

    @pl.when(z == 0)
    def _():
        for back in range(1, REACH + 1):
            @pl.when(y + back < n_rows)
            def _():
                row_copy(back).wait_send()

        all_of(carry_out, carry_sems).wait_send()


def on_device(n_ctx, query, keyed, valued, short_taps, rates, residues, skip_gain, doc_ids):
    block, channels = query.shape
    modes = rates.shape[0]
    assert channels == GROUPS * LANES and block % CHUNK == 0 and modes == 8
    pitch = block + 8
    tile, twice = (GROUPS, LANES), (2 * GROUPS, LANES)
    dma = pltpu.SemaphoreType.DMA
    hbm = pl.BlockSpec(memory_space=pltpu.HBM)
    return pl.pallas_call(
        functools.partial(kernel, n_ctx, pitch),
        out_shape=pltpu.VMEM(query.shape, BF16),
        in_specs=[hbm] * 8,
        out_specs=pl.BlockSpec(memory_space=pltpu.VMEM),
        scratch_shapes=[
            pltpu.VMEM((3, block, channels), BF16),
            pltpu.VMEM((3, GROUPS * pitch, LANES), F32),
            pltpu.VMEM(short_taps.shape, F32),
            pltpu.VMEM(rates.shape, F32),
            pltpu.VMEM(residues.shape, F32),
            pltpu.VMEM(tile, F32),
            pltpu.SMEM((block,), jnp.int32),
            pltpu.VMEM((GROUPS * 32, LANES), F32),
            pltpu.VMEM((9, *tile), F32),
            pltpu.VMEM((modes, *tile), F32),
            pltpu.VMEM((modes, *tile), F32),
            pltpu.VMEM((4, modes, *tile), F32),
            pltpu.VMEM((block, *tile), F32),
            pltpu.VMEM((block, *tile), F32),
            pltpu.VMEM((block, *tile), F32),
            pltpu.VMEM((GROUPS * pitch, LANES), F32),
            pltpu.VMEM((3, *twice), BF16),
            pltpu.VMEM((3, *twice), BF16),
            pltpu.VMEM((1, *twice), BF16),
            pltpu.VMEM((1, *twice), BF16),
            pltpu.VMEM((4, *twice), BF16),
            pltpu.VMEM((4, *twice), BF16),
            pltpu.VMEM((modes + 1, *tile), F32),
            pltpu.VMEM((ROW - 1, modes + 1, *tile), F32),
            pltpu.VMEM((modes + 1, *tile), F32),
            pltpu.VMEM((modes + 1, *tile), F32),
            pltpu.VMEM((modes + 1, *tile), F32),
            pltpu.VMEM((REACH, modes + 1, *tile), F32),
            pltpu.VMEM((ROW - 1, modes, *tile), F32),
            pltpu.VMEM((modes, *tile), F32),
            dma((8,)),
            dma((2,)),
            dma((2,)),
            dma((2,)),
            dma((2,)),
            dma((2,)),
            dma((REACH,)),
            dma((REACH,)),
            dma((2,)),
        ],
        compiler_params=pltpu.CompilerParams(
            collective_id=0, has_side_effects=True, vmem_limit_bytes=60 * 1024 * 1024
        ),
    )(
        query, keyed, valued, short_taps, rates, residues,
        skip_gain.reshape(tile), doc_ids,
    )


def solution(mesh):
    return jax.shard_map(
        functools.partial(on_device, mesh.shape["ctx"]),
        mesh=mesh,
        in_specs=(
            P("ctx", "tp"),
            P("ctx", "tp"),
            P("ctx", "tp"),
            P(None, None, "tp"),
            P(None, "tp"),
            P(None, "tp"),
            P("tp"),
            P("ctx"),
        ),
        out_specs=P("ctx", "tp"),
        check_vma=False,
    )
```

```python
import functools

import jax
import jax.numpy as jnp
from jax import lax
from jax.experimental import pallas as pl
from jax.experimental.pallas import tpu as pltpu
from jax.sharding import PartitionSpec as P

MESH = pl.DeviceIdType.MESH
F32 = jnp.float32
BF16 = jnp.bfloat16
ROW = 8
REACH = 4
LANES = 128
GROUPS = 8
STEP = 32
CHUNK = 128
SPLIT = 4


def tree_sum(terms):
    while len(terms) > 1:
        terms = [a + b for a, b in zip(terms[::2], terms[1::2])] + terms[len(terms) & ~1 :]
    return terms[0]


def flag(cond):
    return jnp.where(cond, 1.0, 0.0).astype(F32)


def kernel(
    n_ctx, pitch,
    q_hbm, k_hbm, v_hbm, taps_hbm, rates_hbm, resid_hbm, skip_hbm, ids_hbm,
    out,
    raw, xs, taps_in, rates_in, resid_in, skip_in, ids,
    prm, taps, rate, resid, power,
    gated, base, live_q, out_x,
    tail_out, tail_in, tail_q_out, tail_q_in, head_out, head_in,
    ends_out, ends_in, relay, relay_in, row_out, row_in, carry_out, carry_in,
    load_sem, tail_sems, tail_q_sems, head_sems, forward_sems, ends_sems,
    row_send, row_recv, carry_sems,
):
    block = q_hbm.shape[0]
    modes = rates_hbm.shape[0]
    last = block - 1
    me = lax.axis_index("ctx")
    tp = lax.axis_index("tp")
    y, z = me // ROW, lax.rem(me, ROW)
    n_rows = n_ctx // ROW
    root = y * ROW

    def at(device):
        return (device, tp)

    def remote(src, dst, send, recv, device):
        return pltpu.make_async_remote_copy(
            src_ref=src, dst_ref=dst, send_sem=send, recv_sem=recv,
            device_id=at(device), device_id_type=MESH,
        )

    barrier = pltpu.get_barrier_semaphore()

    def greet(device):
        pl.semaphore_signal(barrier, inc=1, device_id=at(device), device_id_type=MESH)

    @pl.when(z == 0)
    def _():
        for peer in range(1, ROW):
            greet(root + peer)
        for back in range(1, REACH + 1):
            @pl.when(y >= back)
            def _():
                greet(root - back * ROW)

    @pl.when(z == SPLIT - 1)
    def _():
        greet(me + 1)

    @pl.when(me > 0)
    def _():
        greet(me - 1)

    loads = [
        pltpu.make_async_copy(src, dst, load_sem.at[i])
        for i, (src, dst) in enumerate(
            [
                (k_hbm, raw.at[1]), (v_hbm, raw.at[2]), (ids_hbm, ids), (rates_hbm, rates_in),
                (taps_hbm, taps_in), (q_hbm, raw.at[0]), (resid_hbm, resid_in),
                (skip_hbm, skip_in),
            ]
        )
    ]
    for load in loads:
        load.start()

    def spread(s):
        for j in range(GROUPS):
            xs[s, pl.ds(j * pitch, block), :] = raw[s, :, j * LANES : (j + 1) * LANES].astype(F32)

    def token(s, t):
        return xs[s, pl.ds(t, GROUPS, stride=pitch), :]

    def splat(value):
        return jnp.full((GROUPS, LANES), value.astype(F32), F32)

    def put(ref, i, first, second):
        ref[i] = jnp.concatenate([first, second], axis=0).astype(BF16)

    def get(ref, i):
        both = ref[i].astype(F32)
        return both[:GROUPS], both[GROUPS:]

    loads[0].wait()
    spread(1)
    loads[1].wait()
    spread(2)
    loads[2].wait()
    id_0, id_1, id_end = splat(ids[0]), splat(ids[1]), splat(ids[last])
    for s in (1, 2):
        put(tail_out, s - 1, token(s, last - 1), token(s, last))
        put(head_out, s - 1, token(s, 0), token(s, 1))
    put(tail_out, 2, splat(ids[last - 1]), id_end)
    put(head_out, 2, id_0, id_1)
    put(head_out, 3, id_end, id_end)

    following = lax.rem(me + 1, n_ctx)
    tail = remote(tail_out, tail_in, tail_sems.at[0], tail_sems.at[1], following)
    tail_q = remote(tail_q_out, tail_q_in, tail_q_sems.at[0], tail_q_sems.at[1], following)

    def enter():
        rows_ahead = jnp.minimum(REACH, n_rows - 1 - y)
        expected = jnp.where(me < n_ctx - 1, 1, 0) + jnp.where(z == 0, rows_ahead, 1)
        pl.semaphore_wait(barrier, expected + jnp.where(z == SPLIT, 1, 0))

        @pl.when(me < n_ctx - 1)
        def _():
            tail.start()

    late = (z == 0) | (z == SPLIT - 1)

    @pl.when(jnp.logical_not(late))
    def _():
        enter()

    loads[3].wait()
    loads[4].wait()
    for j in range(GROUPS):
        cols = slice(j * LANES, (j + 1) * LANES)
        prm[pl.ds(j * 32, modes), :] = rates_in[:, cols]
        for s in range(3):
            for tap in range(3):
                prm[pl.ds(j * 32 + 16 + 3 * s + tap, 1), :] = taps_in[s, pl.ds(tap, 1), cols]
    for n in range(modes):
        rate[n] = prm[pl.ds(n, GROUPS, stride=32), :]
        power[0, n] = jnp.exp(-rate[n])
    for i in range(9):
        taps[i] = prm[pl.ds(16 + i, GROUPS, stride=32), :]

    def ends_step(i, carry):
        k1, k2, v1, v2, *state = carry
        decay = [power[0, n] for n in range(modes)]
        t0 = i * STEP
        for d in range(STEP):
            t = t0 + d
            here = ids[t]
            same1 = flag(here == ids[jnp.maximum(t - 1, 0)])
            same2 = flag(here == ids[jnp.maximum(t - 2, 0)])
            ends = flag((here == ids[last]) & (t >= 2))
            k0, v0 = token(1, t), token(2, t)
            kc = taps[3] * k0 + taps[4] * (k1 * same1) + taps[5] * (k2 * same2)
            vc = taps[6] * v0 + taps[7] * (v1 * same1) + taps[8] * (v2 * same2)
            g = (kc * vc).astype(BF16).astype(F32)
            gated[t] = g
            g = g * ends
            state = [decay[n] * state[n] + g for n in range(modes)]
            k1, k2, v1, v2 = k0, k1, v0, v1
        return (k1, k2, v1, v2, *state)

    zero = jnp.zeros((GROUPS, LANES), F32)
    _, _, _, _, *state = lax.fori_loop(0, block // STEP, ends_step, (zero,) * (4 + modes))
    for n in range(modes):
        ends_out[n] = state[n]
    ends_out[modes] = zero
    for i, steps in ((1, block - 2), (2, block), (3, ROW * block)):
        for n in range(modes):
            power[i, n] = jnp.exp(-rate[n] * float(steps))

    @pl.when(late)
    def _():
        enter()

    lifter = root + SPLIT - 1
    head = remote(head_out, head_in, head_sems.at[0], head_sems.at[1], lifter)
    forward = remote(relay, relay_in, forward_sems.at[0], forward_sems.at[1], root)
    slot = lax.rem(z + ROW - 1, ROW)
    ends = remote(ends_out, ends_in.at[slot], ends_sems.at[0], ends_sems.at[1], root)

    @pl.when(z == SPLIT)
    def _():
        head.start()
        ends.start()

    def first_two(s, before, x0, x1, before_ids, id0, id1):
        far, near = before
        id_far, id_near = before_ids
        a, b, c = taps[3 * s], taps[3 * s + 1], taps[3 * s + 2]
        return (
            a * x0 + b * (near * flag(id_near == id0)) + c * (far * flag(id_far == id0)),
            a * x1 + b * (x0 * flag(id0 == id1)) + c * (near * flag(id_near == id1)),
        )

    def first_gated(tail_ref, xk, xv, id0, id1):
        before_ids = get(tail_ref, 2)
        k = first_two(1, get(tail_ref, 0), *xk, before_ids, id0, id1)
        v = first_two(2, get(tail_ref, 1), *xv, before_ids, id0, id1)
        return [(a * b).astype(BF16).astype(F32) for a, b in zip(k, v)]

    def add_first(ref, g, id_near, id0, id1, end_id):
        joined, ending = flag(id0 == id1), flag(id1 == end_id)
        for n in range(modes):
            first = power[0, n] * (g[0] * joined) + g[1]
            ref[n] += power[1, n] * (first * ending)
        ref[modes] = flag(id_near == id0) * flag(id0 == end_id)

    def own_first():
        _, near_id = get(tail_in, 2)
        xk, xv = [(token(s, 0), token(s, 1)) for s in (1, 2)]
        gated[0], gated[1] = g = first_gated(tail_in, xk, xv, id_0, id_1)
        return g, near_id, id_0, id_1, id_end

    prompt = (z != 0) & (z != SPLIT)

    @pl.when(prompt)
    def _():
        tail.wait_recv()
        add_first(ends_out, *own_first())
        ends.start()

    loads[5].wait()
    spread(0)
    put(tail_q_out, 0, token(0, last - 1), token(0, last))

    @pl.when(me < n_ctx - 1)
    def _():
        tail_q.start()

    loads[6].wait()
    loads[7].wait()
    for j in range(GROUPS):
        prm[pl.ds(j * 32 + 8, modes), :] = resid_in[:, j * LANES : (j + 1) * LANES]
    for n in range(modes):
        resid[n] = prm[pl.ds(8 + n, GROUPS, stride=32), :]

    def local_step(i, carry):
        q1, q2, *state = carry
        decay = [power[0, n] for n in range(modes)]
        weight = [resid[n] for n in range(modes)]
        t0 = i * STEP
        for d in range(STEP):
            t = t0 + d
            here = ids[t]
            same1 = flag(here == ids[jnp.maximum(t - 1, 0)])
            same2 = flag(here == ids[jnp.maximum(t - 2, 0)])
            q0 = token(0, t)
            qc = taps[0] * q0 + taps[1] * (q1 * same1) + taps[2] * (q2 * same2)
            g = gated[t]
            if d < 2:
                g = g * flag(t >= 2)
            state = [decay[n] * (state[n] * same1) + g for n in range(modes)]
            long = tree_sum([weight[n] * state[n] for n in range(modes)])
            base[t] = qc * (long + skip_in[...] * g)
            live_q[t] = qc * flag(here == ids[1])
            q1, q2 = q0, q1
        return (q1, q2, *state)

    lax.fori_loop(0, block // STEP, local_step, (zero,) * (2 + modes))

    @pl.when((z == SPLIT) | ((z == 0) & (me > 0)))
    def _():
        tail.wait_recv()

    @pl.when(me == 0)
    def _():
        tail_in[...] = jnp.full(tail_in.shape, -1.0, BF16)
        tail_q_in[...] = jnp.zeros(tail_q_in.shape, BF16)

    @pl.when(z == 0)
    def _():
        add_first(ends_out, *own_first())

    @pl.when(z == SPLIT)
    def _():
        own_first()

    @pl.when(z == SPLIT - 1)
    def _():
        head.wait_recv()
        relay[...] = jnp.zeros(relay.shape, F32)
        (head_0, head_1), (head_end, _) = get(head_in, 2), get(head_in, 3)
        first = first_gated(tail_out, get(head_in, 0), get(head_in, 1), head_0, head_1)
        add_first(relay, first, id_end, head_0, head_1, head_end)
        forward.start()

    @pl.when(me > 0)
    def _():
        tail_q.wait_recv()

    def row_copy(back):
        return remote(
            row_out.at[pl.ds(0, modes + (back < REACH))],
            row_in.at[back - 1, pl.ds(0, modes + (back < REACH))],
            row_send.at[back - 1], row_recv.at[back - 1],
            lax.rem(me + back * ROW, n_ctx),
        )

    def carry_copy(peer):
        return remote(
            carry_out.at[peer - 1], carry_in, carry_sems.at[0], carry_sems.at[1], root + peer
        )

    def all_of(ref, sems):
        return remote(ref, ref, sems.at[0], sems.at[1], root)

    @pl.when(z == 0)
    def _():
        forward.wait_recv()
        all_of(ends_in, ends_sems).wait_recv()
        for n in range(modes + 1):
            ends_in[SPLIT - 1, n] += relay_in[n]
        hop = [power[2, n] for n in range(modes)]
        leap = [power[3, n] for n in range(modes)]
        total = [ends_out[n] for n in range(modes)]
        keep = ends_out[modes]
        for peer in range(1, ROW):
            k = ends_in[peer - 1, modes]
            keep = keep * k
            total = [total[n] * (hop[n] * k) + ends_in[peer - 1, n] for n in range(modes)]
        for n in range(modes):
            row_out[n] = total[n]
        row_out[modes] = keep

        orders = {0: (1, 2, 3, 4), 1: (1, 2, 4, 3), 2: (4, 1, 3, 2), 3: (4, 3, 2, 1)}
        for at_row in range(n_rows):
            @pl.when(y == at_row)
            def _():
                for back in orders.get(at_row, (3, 2, 1)):
                    if at_row + back < n_rows:
                        row_copy(back).start()

        carry_in[...] = jnp.zeros(carry_in.shape, F32)
        for back in range(REACH, 0, -1):
            @pl.when(y >= back)
            def _():
                row_copy(back).wait_recv()
                for n in range(modes):
                    if back == REACH:
                        carry_in[n] = row_in[back - 1, n]
                    else:
                        carry_in[n] = (
                            leap[n] * row_in[back - 1, modes] * carry_in[n] + row_in[back - 1, n]
                        )

        now = [carry_in[n] for n in range(modes)]
        for peer in range(1, ROW):
            src = ends_out if peer == 1 else ends_in.at[peer - 2]
            k = src[modes]
            now = [now[n] * (hop[n] * k) + src[n] for n in range(modes)]
            for n in range(modes):
                carry_out[peer - 1, n] = now[n]
            carry_copy(peer).start()

    @pl.when(z > 0)
    def _():
        carry_copy(1).wait_recv()

    before_ids = get(tail_in, 2)
    q_first = first_two(0, get(tail_q_in, 0), token(0, 0), token(0, 1), before_ids, id_0, id_1)
    state = [carry_in[n] * flag(before_ids[1] == id_0) for n in range(modes)]
    for t in (0, 1):
        if t == 1:
            joined = flag(id_0 == id_1)
            state = [state[n] * joined for n in range(modes)]
        state = [power[0, n] * state[n] + gated[t] for n in range(modes)]
        long = tree_sum([resid[n] * state[n] for n in range(modes)])
        base[t] = q_first[t] * (long + skip_in[...] * gated[t])
        live_q[t] = zero

    def out_step(c, part):
        decay = [power[0, n] for n in range(modes)]
        for d in range(CHUNK):
            t = c * CHUNK + d
            part = [decay[n] * part[n] for n in range(modes)]
            out_x[pl.ds(t, GROUPS, stride=pitch), :] = base[t] + live_q[t] * tree_sum(list(part))
        for j in range(GROUPS):
            rows = pl.ds(pl.multiple_of(c * CHUNK, CHUNK), CHUNK)
            piece = out_x[pl.ds(j * pitch + pl.multiple_of(c * CHUNK, CHUNK), CHUNK), :]
            out[rows, j * LANES : (j + 1) * LANES] = piece.astype(BF16)
        return part

    lax.fori_loop(
        0, block // CHUNK, out_step, [resid[n] * jnp.exp(2.0 * rate[n]) * state[n] for n in range(modes)]
    )

    @pl.when(me < n_ctx - 1)
    def _():
        tail.wait_send()
        tail_q.wait_send()

    @pl.when(z == SPLIT - 1)
    def _():
        forward.wait_send()

    @pl.when(z == SPLIT)
    def _():
        head.wait_send()

    @pl.when(z > 0)
    def _():
        ends.wait_send()

    @pl.when(z == 0)
    def _():
        for back in range(1, REACH + 1):
            @pl.when(y + back < n_rows)
            def _():
                row_copy(back).wait_send()

        all_of(carry_out, carry_sems).wait_send()


def on_device(n_ctx, query, keyed, valued, short_taps, rates, residues, skip_gain, doc_ids):
    block, channels = query.shape
    modes = rates.shape[0]
    assert channels == GROUPS * LANES and block % CHUNK == 0 and modes == 8
    pitch = block + 8
    tile, twice = (GROUPS, LANES), (2 * GROUPS, LANES)
    dma = pltpu.SemaphoreType.DMA
    hbm = pl.BlockSpec(memory_space=pltpu.HBM)
    return pl.pallas_call(
        functools.partial(kernel, n_ctx, pitch),
        out_shape=pltpu.VMEM(query.shape, BF16),
        in_specs=[hbm] * 8,
        out_specs=pl.BlockSpec(memory_space=pltpu.VMEM),
        scratch_shapes=[
            pltpu.VMEM((3, block, channels), BF16),
            pltpu.VMEM((3, GROUPS * pitch, LANES), F32),
            pltpu.VMEM(short_taps.shape, F32),
            pltpu.VMEM(rates.shape, F32),
            pltpu.VMEM(residues.shape, F32),
            pltpu.VMEM(tile, F32),
            pltpu.SMEM((block,), jnp.int32),
            pltpu.VMEM((GROUPS * 32, LANES), F32),
            pltpu.VMEM((9, *tile), F32),
            pltpu.VMEM((modes, *tile), F32),
            pltpu.VMEM((modes, *tile), F32),
            pltpu.VMEM((4, modes, *tile), F32),
            pltpu.VMEM((block, *tile), F32),
            pltpu.VMEM((block, *tile), F32),
            pltpu.VMEM((block, *tile), F32),
            pltpu.VMEM((GROUPS * pitch, LANES), F32),
            pltpu.VMEM((3, *twice), BF16),
            pltpu.VMEM((3, *twice), BF16),
            pltpu.VMEM((1, *twice), BF16),
            pltpu.VMEM((1, *twice), BF16),
            pltpu.VMEM((4, *twice), BF16),
            pltpu.VMEM((4, *twice), BF16),
            pltpu.VMEM((modes + 1, *tile), F32),
            pltpu.VMEM((ROW - 1, modes + 1, *tile), F32),
            pltpu.VMEM((modes + 1, *tile), F32),
            pltpu.VMEM((modes + 1, *tile), F32),
            pltpu.VMEM((modes + 1, *tile), F32),
            pltpu.VMEM((REACH, modes + 1, *tile), F32),
            pltpu.VMEM((ROW - 1, modes, *tile), F32),
            pltpu.VMEM((modes, *tile), F32),
            dma((8,)),
            dma((2,)),
            dma((2,)),
            dma((2,)),
            dma((2,)),
            dma((2,)),
            dma((REACH,)),
            dma((REACH,)),
            dma((2,)),
        ],
        compiler_params=pltpu.CompilerParams(
            collective_id=0, has_side_effects=True, vmem_limit_bytes=60 * 1024 * 1024
        ),
    )(
        query, keyed, valued, short_taps, rates, residues,
        skip_gain.reshape(tile), doc_ids,
    )


def solution(mesh):
    return jax.shard_map(
        functools.partial(on_device, mesh.shape["ctx"]),
        mesh=mesh,
        in_specs=(
            P("ctx", "tp"),
            P("ctx", "tp"),
            P("ctx", "tp"),
            P(None, None, "tp"),
            P(None, "tp"),
            P(None, "tp"),
            P("tp"),
            P("ctx"),
        ),
        out_specs=P("ctx", "tp"),
        check_vma=False,
    )
```
